512 devices in a mesh: grp: 16 (over x, y), mlp: 32 (over z, core).
Axes of the slice: x: 4, y: 4, z: 16, core: 2. Of those that a mesh axis runs over, the one named last changes fastest.
Arguments:
- queries: bfloat16 [65536, 4096], P(('grp', 'mlp')), may hold values from -8 to 8
- keys: bfloat16 [65536, 4096], P(('grp', 'mlp')), may hold values from -8 to 8
- values: bfloat16 [65536, 4096], P(('grp', 'mlp')), may hold values from -6 to 6
- gamma: bfloat16 [4096], P('mlp'), may hold values from 0.25 to 2
- w_merge: bfloat16 [4096, 4096], P('grp', 'mlp'), may hold values from -0.09375 to 0.09375
- grids: int32 [256, 2], P('grp'), may hold values from 8 to 16, as said below
- positions: int32 [16384], replicated, may hold values from 0 to 16383, as said below
Outputs:
- prompt_embeds: bfloat16 [16384, 4096], P('grp', 'mlp')
The draws below stay inside these ranges and needn't reach their ends.
Inputs may be any that keep to these rules, and one draw needn't show every extreme that they name: `grids`: every grid side is even and at least 8; each group has an image of 16 x 16, and a group's images fill at most 4096 slots. positions is a permutation. From one group's 1024 slots at most 128 go to one block of 1024 consecutive prompt positions, and exactly 128 go to some block.
All inputs are finite; a program needn't handle non-finite values.
Results may differ from the reference program's by a relative error of at most 0.015.
Values may be sent and summed in bfloat16 or wider, within the bound.
No kernel may reach another device: no remote copies, remote signals or barrier semaphores. Data moves between devices by JAX's collectives and lax.ppermute only.
A program may use at most 64 MiB of HBM per device.

```python
import math
import jax
import jax.numpy as jnp
import numpy as np
from jax import lax

HEADS = 32
HD = 128
D = 4096
GRID = 16
GTOK = 4096
IMGS = 16
GPOOL = 1024
CAP = 128
TOKENS = 65536
PROMPT = 16384
QB = 512


def query_key_pair(key):
    shape = (TOKENS, D)
    first = jnp.clip(jax.random.normal(jax.random.fold_in(key, 11), shape, jnp.float32), -6.0, 6.0)
    second = jnp.clip(jax.random.normal(jax.random.fold_in(key, 12), shape, jnp.float32), -6.0, 6.0)
    return (first, second)


def draw_queries(key, part):
    return query_key_pair(key)[0].astype(jnp.bfloat16)


def draw_keys(key, part):
    return query_key_pair(key)[1].astype(jnp.bfloat16)


def draw_grids(key, part):
    groups = TOKENS // (IMGS * GRID * GRID)
    halves = jax.random.randint(jax.random.fold_in(key, 1), (groups * IMGS, 2), GRID // 4, GRID // 2 + 1) * 2
    largest = jax.random.randint(jax.random.fold_in(key, 2), (groups,), 0, IMGS)
    forced = (jnp.arange(IMGS)[None, :] == largest[:, None]).reshape(-1)
    return jnp.where(forced[:, None], GRID, halves).astype(jnp.int32)


def draw_positions(key, part):
    block = GPOOL
    blocks = PROMPT // GPOOL
    rest = block - CAP
    even = rest // (blocks - 1)
    extra = rest % (blocks - 1)
    counts = np.array([CAP] + [even + (1 if o < extra else 0) for o in range(blocks - 1)], dtype=np.int32)
    ends = np.cumsum(counts).astype(np.int32)
    begins = (ends - counts).astype(np.int32)
    offsets_before = np.zeros((blocks, blocks), dtype=np.int32)
    for group in range(blocks):
        for target in range(blocks):
            offsets_before[group, target] = sum((int(counts[(target - other) % blocks]) for other in range(group)))
    labels = jax.random.permutation(jax.random.fold_in(key, 21), blocks)
    row_keys = jax.random.split(jax.random.fold_in(key, 22), blocks)
    ranks = jax.vmap(lambda k: jax.random.permutation(k, block))(row_keys)
    offset = jnp.sum((ranks[:, :, None] >= jnp.asarray(ends)[None, None, :]).astype(jnp.int32), axis=-1)
    within = ranks - jnp.asarray(begins)[offset]
    group_ids = jnp.arange(blocks, dtype=jnp.int32)[:, None]
    target = (offset + group_ids) % blocks
    dest = labels[target]
    raw = jnp.asarray(offsets_before)[group_ids, target] + within
    slot_keys = jax.random.split(jax.random.fold_in(key, 23), blocks)
    slot_perm = jax.vmap(lambda k: jax.random.permutation(k, block))(slot_keys)
    slot = slot_perm[dest, raw]
    return (dest * block + slot).reshape(-1).astype(jnp.int32)


def block_scale(own_key, dims, pieces, low, top_value):
    level = 1.0
    for axis_at, parts in pieces:
        steps = jax.random.uniform(jax.random.fold_in(jax.random.fold_in(own_key, 6), axis_at), (parts,), jnp.float32, low / len(pieces), top_value / len(pieces))
        level = level * jnp.repeat(jnp.exp(steps), dims[axis_at] // parts).reshape((-1,) + (1,) * (len(dims) - 1 - axis_at))
    return level


def bell_draw(rng, shape, deviation, bound, shards=(), kind=jnp.bfloat16):
    entries = deviation * jax.random.normal(rng, shape, jnp.float32)
    if shards:
        entries = entries * block_scale(rng, shape, shards, -0.22, 0.18)
    return jnp.clip(entries, -bound, bound).astype(kind)


def setup_inputs(seed: int = 0) -> dict:
    arg_keys = jax.random.split(jax.random.key(seed), 8)
    return {
        "queries": draw_queries(jax.random.fold_in(arg_keys[7], 71), 0),
        "keys": draw_keys(jax.random.fold_in(arg_keys[7], 71), 0),
        "values": bell_draw(arg_keys[2], (TOKENS, D), 1.0, 6.0, ((0, 512),)),
        "gamma": jnp.clip(jnp.exp(math.log(2.0) - 2.0794415 * jax.random.uniform(arg_keys[3], (D,), jnp.float32) ** block_scale(arg_keys[3], (D,), ((0, 32),), -0.2, 0.2)), 0.25, 2.0).astype(jnp.bfloat16),
        "w_merge": bell_draw(arg_keys[4], (D, D), D ** -0.5, 0.09375, ((0, 16), (1, 32))),
        "grids": draw_grids(jax.random.fold_in(arg_keys[7], 71), 0),
        "positions": draw_positions(jax.random.fold_in(arg_keys[7], 71), 0),
    }


def token_layout(grid, gtok):
    heights = grid[:, 0]
    widths = grid[:, 1]
    areas = heights * widths
    ends = jnp.cumsum(areas).astype(jnp.int32)
    starts = (ends - areas).astype(jnp.int32)
    count = grid.shape[0]
    slots = jnp.arange(gtok, dtype=jnp.int32)
    image = jnp.sum((slots[:, None] >= ends[None, :]).astype(jnp.int32), axis=1)
    starts_ext = jnp.concatenate([starts, ends[-1:]]).astype(jnp.int32)
    widths_ext = jnp.concatenate([widths, jnp.full((1,), 2, jnp.int32)]).astype(jnp.int32)
    onehot = (image[:, None] == jnp.arange(count + 1, dtype=jnp.int32)[None, :]).astype(jnp.int32)
    first = jnp.sum(onehot * starts_ext[None, :], axis=1)
    width = jnp.sum(onehot * widths_ext[None, :], axis=1)
    local = slots - first
    return image, local // width, local % width


def pool_layout(grid, gpool):
    heights = grid[:, 0]
    widths = grid[:, 1]
    areas = heights * widths
    ends = jnp.cumsum(areas).astype(jnp.int32)
    starts = (ends - areas).astype(jnp.int32)
    count = grid.shape[0]
    slots = jnp.arange(gpool, dtype=jnp.int32)
    image = jnp.sum((slots[:, None] >= (ends // 4)[None, :]).astype(jnp.int32), axis=1)
    starts_ext = jnp.concatenate([starts, ends[-1:]]).astype(jnp.int32)
    widths_ext = jnp.concatenate([widths, jnp.full((1,), 2, jnp.int32)]).astype(jnp.int32)
    onehot = (image[:, None] == jnp.arange(count + 1, dtype=jnp.int32)[None, :]).astype(jnp.int32)
    first = jnp.sum(onehot * starts_ext[None, :], axis=1)
    width = jnp.sum(onehot * widths_ext[None, :], axis=1)
    local = slots - first // 4
    half = width // 2
    anchor = first + 2 * (local // half) * width + 2 * (local % half)
    sources = jnp.stack([anchor, anchor + 1, anchor + width, anchor + width + 1], axis=1)
    sources = jnp.clip(sources, 0, 4 * gpool - 1).astype(jnp.int32)
    return sources, image < count


def rotate(block, row, col):
    quarter = block.shape[2] // 4
    freq = 100.0 ** (-jnp.arange(quarter, dtype=jnp.float32) / quarter)
    ang_row = row.astype(jnp.float32)[:, None, None] * freq[None, None, :]
    ang_col = col.astype(jnp.float32)[:, None, None] * freq[None, None, :]
    full = block.astype(jnp.float32)
    first = full[..., :quarter]
    second = full[..., quarter:2 * quarter]
    third = full[..., 2 * quarter:3 * quarter]
    fourth = full[..., 3 * quarter:]
    out = jnp.concatenate([
        first * jnp.cos(ang_row) - second * jnp.sin(ang_row),
        second * jnp.cos(ang_row) + first * jnp.sin(ang_row),
        third * jnp.cos(ang_col) - fourth * jnp.sin(ang_col),
        fourth * jnp.cos(ang_col) + third * jnp.sin(ang_col)], axis=-1)
    return out.astype(jnp.bfloat16)


def attend(rot_q, rot_k, vals, image, qrows, margin):
    gtok = rot_q.shape[0]
    scale = rot_q.shape[2] ** -0.5
    pad_k = jnp.pad(rot_k, ((margin, margin), (0, 0), (0, 0)))
    pad_v = jnp.pad(vals, ((margin, margin), (0, 0), (0, 0)))
    pad_id = jnp.pad(image, (margin, margin), constant_values=-1)

    def block(index):
        start = index * qrows
        q_blk = lax.dynamic_slice_in_dim(rot_q, start, qrows, 0)
        k_blk = lax.dynamic_slice_in_dim(pad_k, start, qrows + 2 * margin, 0)
        v_blk = lax.dynamic_slice_in_dim(pad_v, start, qrows + 2 * margin, 0)
        q_ids = lax.dynamic_slice_in_dim(image, start, qrows, 0)
        k_ids = lax.dynamic_slice_in_dim(pad_id, start, qrows + 2 * margin, 0)
        scores = jnp.einsum("qhd,khd->hqk", q_blk.astype(jnp.float32), k_blk.astype(jnp.float32)) * scale
        keep = q_ids[:, None] == k_ids[None, :]
        scores = jnp.where(keep[None, :, :], scores, -1e30)
        top = jnp.max(scores, axis=-1, keepdims=True)
        expo = jnp.exp(scores - top)
        probs = (expo / jnp.sum(expo, axis=-1, keepdims=True)).astype(jnp.bfloat16)
        return jnp.einsum("hqk,khd->qhd", probs.astype(jnp.float32), v_blk.astype(jnp.float32))

    outs = lax.map(block, jnp.arange(gtok // qrows, dtype=jnp.int32))
    return outs.reshape(gtok, rot_q.shape[1], rot_q.shape[2])


def reference(queries, keys, values, gamma, w_merge, grids, positions):
    groups = TOKENS // GTOK
    q_all = queries.reshape(groups, GTOK, HEADS, HD)
    k_all = keys.reshape(groups, GTOK, HEADS, HD)
    v_all = values.reshape(groups, GTOK, HEADS, HD)
    g_all = grids.reshape(groups, IMGS, 2)
    gains = gamma.astype(jnp.float32).reshape(HEADS, HD)

    def per_group(items):
        q_grp, k_grp, v_grp, grid = items
        image, row, col = token_layout(grid, GTOK)
        rot_q = rotate(q_grp, row, col)
        rot_k = rotate(k_grp, row, col)
        attn = attend(rot_q, rot_k, v_grp, image, QB, GRID * GRID)
        branch = (attn * gains[None, :, :]).astype(jnp.bfloat16).reshape(GTOK, D)
        sources, valid = pool_layout(grid, GPOOL)
        picked = jnp.take(branch, sources, axis=0).astype(jnp.float32)
        pooled = jnp.where(valid[:, None], 0.25 * jnp.sum(picked, axis=1), 0.0)
        return pooled.astype(jnp.bfloat16)

    pooled = lax.map(per_group, (q_all, k_all, v_all, g_all)).reshape(PROMPT, D)
    merged = jnp.dot(pooled, w_merge, preferred_element_type=jnp.float32).astype(jnp.bfloat16)
    return jnp.zeros((PROMPT, D), jnp.bfloat16).at[positions].set(merged)
```

```python
import functools
import math

import jax
import jax.numpy as jnp
from jax import lax
from jax.experimental import pallas as pl
from jax.experimental.pallas import tpu as pltpu
from jax.sharding import PartitionSpec as P

HD = 128
HALF = 2048
IMGS = 16
BLK = 128
CHIPS = 16
NB = 4
ROWS = 64
CAP = 128
GROUPS = 16
GPOOL = 1024
NEG = -1e30
F32 = jnp.float32
BF16 = jnp.bfloat16
I32 = jnp.int32


def at(z, c):
    return (z % CHIPS) * 2 + c


SAME = [(at(z, 0), at(z - 1, 0)) for z in range(CHIPS)] + [(at(z, 1), at(z + 1, 1)) for z in range(CHIPS)]
OPP = [(at(z, 1), at(z - 1, 0)) for z in range(CHIPS)] + [(at(z, 0), at(z + 1, 1)) for z in range(CHIPS)]
RING = [(at(z, 0), at(z + 1, 0)) for z in range(CHIPS)] + [(at(z, 1), at(z - 1, 1)) for z in range(CHIPS)]
PART = [(at(z, c), at(z, 1 - c)) for z in range(CHIPS) for c in range(2)]


def vmem():
    return pl.BlockSpec(memory_space=pltpu.VMEM)


def smem():
    return pl.BlockSpec(memory_space=pltpu.SMEM)


def params(mib):
    return pltpu.CompilerParams(vmem_limit_bytes=mib << 20)


def images_of(tok, grid_ref):
    image = jnp.where(tok < 0, -1, 0)
    first = jnp.zeros_like(tok)
    width = jnp.full_like(tok, grid_ref[0, 1])
    end = jnp.full_like(tok, grid_ref[0, 0] * grid_ref[0, 1])
    upto = jnp.int32(0)
    for n in range(IMGS):
        upto = upto + grid_ref[n, 0] * grid_ref[n, 1]
        past = tok >= upto
        image = jnp.where(past, n + 1, image)
        first = jnp.where(past, upto, first)
        if n + 1 < IMGS:
            width = jnp.where(past, grid_ref[n + 1, 1], width)
            end = jnp.where(past, upto + grid_ref[n + 1, 0] * grid_ref[n + 1, 1], end)
        else:
            width = jnp.where(past, 2, width)
    return image, first, width, end


def divide(a, b):
    return jnp.floor((a.astype(F32) + 0.5) / b.astype(F32)).astype(I32)


def rope_kernel(scal_ref, grid_ref, q_ref, k_ref, v_ref, own_ref, oth_ref):
    core = scal_ref[1]
    base = scal_ref[0] * BLK
    tok = base + lax.broadcasted_iota(I32, (BLK, HD), 0)
    lane = lax.broadcasted_iota(I32, (BLK, HD), 1)
    _, first, width, _ = images_of(tok, grid_ref)
    local = tok - first
    row = divide(local, width)
    col = local - row * width
    k = (lane % 32).astype(F32)
    freq = jnp.exp(k * (-math.log(100.0) / 32.0))
    ang = jnp.where(lane < 64, row, col).astype(F32) * freq
    cos = jnp.cos(ang)
    low = (lane % 64) < 32
    sin = jnp.where(low, -jnp.sin(ang), jnp.sin(ang))
    for out_ref, half in ((own_ref, core), (oth_ref, 1 - core)):

        def head(h, carry, out_ref=out_ref, half=half):
            src = pl.multiple_of(half * HALF + h * HD, HD)
            dst = pl.multiple_of(h * HD, HD)
            for i, ref in ((0, q_ref), (1, k_ref)):
                x = ref[:, pl.ds(src, HD)].astype(F32)
                swap = jnp.where(low, pltpu.roll(x, 96, 1), pltpu.roll(x, 32, 1))
                out_ref[i, :, pl.ds(dst, HD)] = (x * cos + swap * sin).astype(BF16)
            out_ref[2, :, pl.ds(dst, HD)] = v_ref[:, pl.ds(src, HD)]
            return carry

        lax.fori_loop(0, HALF // HD, head, 0)


def attend_kernel(scal_ref, grid_ref, a_ref, b_ref, c_ref, d_ref, gamma_ref, mid_ref, edge_ref, bias_ref, pool_ref):
    chip = scal_ref[0] // 2
    core = scal_ref[1]
    lo = chip * 2 * BLK
    hi = lo + 2 * BLK

    @pl.when(pl.program_id(0) == 0)
    def _():
        lane = lax.broadcasted_iota(I32, (8, NB * BLK), 1)
        place = lane // BLK
        ktok = lo + lane % BLK + BLK * jnp.where(core == 0, place, 1 - place)
        kimg, kfirst, kwidth, kend = images_of(ktok, grid_ref)
        for i in range(NB):
            qtok = lo + BLK * jnp.where(core == 0, i, 1 - i) + lax.broadcasted_iota(I32, (BLK, HD), 0)
            qimg, _, _, _ = images_of(qtok, grid_ref)
            for j in range(NB):
                same = qimg == kimg[:1, j * BLK : (j + 1) * BLK]
                bias_ref[i * BLK : (i + 1) * BLK, j * BLK : (j + 1) * BLK] = jnp.where(same, 0.0, NEG)
        local = ktok - kfirst
        prow = divide(jnp.maximum(local, 0), kwidth)
        pcol = local - prow * kwidth
        target = kfirst // 4 + (prow // 2) * (kwidth // 2) + pcol // 2
        begins = (kfirst >= lo) & (kfirst < hi)
        ends = (kend > lo) & (kend <= hi)
        owned = jnp.where(core == 0, begins.astype(I32), ends.astype(I32)) > 0
        valid = owned & (kimg >= 0) & (kimg < IMGS)
        target = jnp.where(valid, target, -1)[:1]
        r = lax.broadcasted_iota(I32, (2 * ROWS, NB * BLK), 0)
        far = jnp.where(core == 0, ROWS, -ROWS)
        mine = chip * ROWS + jnp.where(r < ROWS, r, r - ROWS + far)
        pool_ref[...] = jnp.where((target == mine) & (target >= 0), 1.0, 0.0).astype(BF16)

    refs = (a_ref, b_ref, c_ref, d_ref)
    keys = jnp.concatenate([ref[1] for ref in refs], axis=0)
    vals = jnp.concatenate([ref[2] for ref in refs], axis=0)
    gamma = gamma_ref[...].astype(F32)
    scale = HD ** -0.5
    branch = []
    for i in range(NB):
        s = lax.dot_general(refs[i][0], keys, (((1,), (1,)), ((), ())), preferred_element_type=F32)
        s = s * scale + bias_ref[i * BLK : (i + 1) * BLK, :]
        e = jnp.exp(s - jnp.max(s, axis=1, keepdims=True))
        total = jnp.sum(e, axis=1, keepdims=True)
        o = jnp.dot(e.astype(BF16), vals, preferred_element_type=F32)
        branch.append((o * (gamma / total)).astype(BF16))
    pooled = 0.25 * jnp.dot(pool_ref[...], jnp.concatenate(branch, axis=0), preferred_element_type=F32)
    pooled = pooled.astype(BF16)
    mid_ref[...] = pooled[:ROWS]
    edge_ref[...] = pooled[ROWS:]


def project_kernel(scal_ref, *refs):
    core = scal_ref[1]
    w_ref = refs[-3]
    mine_ref, send_ref = refs[-2:]
    n = (len(refs) - 3) // 2
    own = jnp.concatenate([refs[2 * i][...] for i in range(n)], axis=0)
    oth = jnp.concatenate([refs[2 * i + 1][...] for i in range(n)], axis=0)
    for side, out_ref in ((0, mine_ref), (1, send_ref)):
        total = jnp.dot(own, w_ref[side, core], preferred_element_type=F32)
        total += jnp.dot(oth, w_ref[side, 1 - core], preferred_element_type=F32)
        out_ref[...] = total.astype(BF16)


def index_kernel(scal_ref, pos_ref, to_ref, from_ref):
    group = scal_ref[2]
    i = lax.broadcasted_iota(I32, (GPOOL, GPOOL), 0)
    j = lax.broadcasted_iota(I32, (GPOOL, GPOOL), 1)
    before = jnp.where(i < j, 1.0, 0.0).astype(BF16)
    own = pos_ref[pl.ds(group, 1), :] // GPOOL
    hot = (own == lax.broadcasted_iota(I32, (GROUPS, GPOOL), 0)).astype(F32)
    count = jnp.dot(hot.astype(BF16), before, preferred_element_type=F32)
    rank = jnp.sum(hot * count, axis=0, keepdims=True)
    to_ref[...] = own * CAP + rank.astype(I32)
    pos = pos_ref[...]
    here = pos // GPOOL == group
    rank = jnp.dot(here.astype(F32).astype(BF16), before, preferred_element_type=F32).astype(I32)
    rank = jnp.where(here, rank, -1)
    local = pos % GPOOL + 1
    high = (local // 32).astype(F32)
    low = (local % 32).astype(F32)
    r = lax.broadcasted_iota(I32, (CAP, GPOOL), 0)
    for g in range(GROUPS):
        pick = (rank[g : g + 1] == r).astype(F32).astype(BF16)
        pair = jnp.concatenate([high[g : g + 1], low[g : g + 1], jnp.zeros((6, GPOOL), F32)], axis=0)
        got = lax.dot_general(pair.astype(BF16), pick, (((1,), (1,)), ((), ())), preferred_element_type=F32)
        value = got[0:1] * 32.0 + got[1:2] - 1.0
        from_ref[:, g * CAP : (g + 1) * CAP] = value.astype(I32)


def send_kernel(scal_ref, to_ref, mine_ref, got_ref, out_ref, all_ref):
    chip = scal_ref[0] // 2
    core = scal_ref[1]
    full = CHIPS // 2 - 1
    half = ROWS // 2
    step = jnp.where(core == 0, CHIPS - 1, 1)

    def put(ref, src, n, row):
        all_ref[pl.ds(pl.multiple_of(row, half), n), :] = ref[src : src + n, :]

    put(mine_ref, 0, ROWS, chip * ROWS)
    for k in range(1, full + 1):
        put(mine_ref, k * ROWS, ROWS, ((chip + k * step) % CHIPS) * ROWS)
        put(got_ref, (k - 1) * ROWS, ROWS, ((chip + k * (CHIPS - step)) % CHIPS) * ROWS)
    last = ((chip + CHIPS // 2) % CHIPS) * ROWS
    put(mine_ref, (full + 1) * ROWS, half, last + core * half)
    put(got_ref, full * ROWS, half, last + (1 - core) * half)
    rows = 256
    for i in range(GROUPS * CAP // rows):
        r = i * rows + lax.broadcasted_iota(I32, (rows, GPOOL), 0)
        pick = jnp.where(to_ref[...] == r, 1.0, 0.0).astype(BF16)
        out_ref[i * rows : (i + 1) * rows, :] = jnp.dot(pick, all_ref[...], preferred_element_type=F32).astype(BF16)


def place_kernel(from_ref, got_ref, out_ref):
    rows = 256
    for i in range(GPOOL // rows):
        r = i * rows + lax.broadcasted_iota(I32, (rows, GROUPS * CAP), 0)
        pick = jnp.where(from_ref[...] == r, 1.0, 0.0).astype(BF16)
        out_ref[i * rows : (i + 1) * rows, :] = jnp.dot(pick, got_ref[...], preferred_element_type=F32).astype(BF16)


def body(queries, keys, values, gamma, w_merge, grids, positions):
    me = lax.axis_index("mlp")
    core = me % 2
    scal = jnp.stack([me, core, lax.axis_index("grp"), me]).astype(I32)
    shape = jax.ShapeDtypeStruct

    own, oth = pl.pallas_call(
        rope_kernel,
        out_shape=[shape((3, BLK, HALF), BF16)] * 2,
        in_specs=[smem(), smem(), vmem(), vmem(), vmem()],
        out_specs=[vmem(), vmem()],
        compiler_params=params(24),
        name="rope",
    )(scal, grids, queries, keys, values)
    up = lax.ppermute(own, "mlp", SAME)
    across = lax.ppermute(oth, "mlp", OPP)
    beside = lax.ppermute(oth, "mlp", PART)

    gains = lax.all_to_all(
        jnp.broadcast_to(gamma[None, :], (2 * CHIPS, HD)), "mlp", split_axis=0, concat_axis=0, tiled=True
    )
    gains = lax.dynamic_slice_in_dim(gains, core * CHIPS, CHIPS, 0).reshape(1, HALF)

    cols = lax.all_gather(w_merge, "grp", axis=0, tiled=True)
    cols = jnp.stack([cols, lax.ppermute(cols, "mlp", PART)]).reshape(2, 2, HALF, HD)

    to, frm = pl.pallas_call(
        index_kernel,
        out_shape=[shape((1, GPOOL), I32), shape((1, GROUPS * CAP), I32)],
        in_specs=[smem(), vmem()],
        out_specs=[vmem(), vmem()],
        compiler_params=params(24),
        name="index",
    )(scal, positions.reshape(GROUPS, GPOOL))

    part = pl.BlockSpec((3, BLK, HD), lambda h: (0, 0, h))
    mid, edge = pl.pallas_call(
        attend_kernel,
        grid=(CHIPS,),
        out_shape=[shape((ROWS, HALF), BF16)] * 2,
        in_specs=[smem(), smem(), part, part, part, part, pl.BlockSpec((1, HD), lambda h: (0, h))],
        out_specs=[pl.BlockSpec((ROWS, HD), lambda h: (0, h))] * 2,
        scratch_shapes=[pltpu.VMEM((NB * BLK, NB * BLK), F32), pltpu.VMEM((2 * ROWS, NB * BLK), BF16)],
        compiler_params=params(24),
        name="attend",
    )(scal, grids, own, beside, up, across, gains)

    h_own = mid + lax.ppermute(edge, "mlp", RING)
    h_oth = lax.ppermute(mid, "mlp", PART) + lax.ppermute(edge, "mlp", OPP)
    shards = [h_own, h_oth]
    a, b = h_own, h_oth
    for _ in range(CHIPS // 2 - 1):
        a = lax.ppermute(a, "mlp", RING)
        b = lax.ppermute(b, "mlp", RING)
        shards += [a, b]
    a = lax.ppermute(lax.dynamic_slice_in_dim(a, core * 32, 32, 0), "mlp", RING)
    b = lax.ppermute(lax.dynamic_slice_in_dim(b, core * 32, 32, 0), "mlp", RING)
    shards += [a, b]

    rows = ROWS * (CHIPS // 2) + ROWS // 2
    mine, send = pl.pallas_call(
        project_kernel,
        out_shape=[shape((rows, HD), BF16)] * 2,
        in_specs=[smem()] + [vmem()] * (len(shards) + 1),
        out_specs=[vmem(), vmem()],
        compiler_params=params(32),
        name="project",
    )(scal, *shards, cols)
    got = lax.ppermute(send[ROWS:], "mlp", PART)
    out = pl.pallas_call(
        send_kernel,
        out_shape=shape((GROUPS * CAP, HD), BF16),
        in_specs=[smem(), vmem(), vmem(), vmem()],
        out_specs=vmem(),
        scratch_shapes=[pltpu.VMEM((GPOOL, HD), BF16)],
        compiler_params=params(24),
        name="pack",
    )(scal, to, mine, got)
    out = lax.all_to_all(out, "grp", split_axis=0, concat_axis=0, tiled=True)
    return pl.pallas_call(
        place_kernel,
        out_shape=shape((GPOOL, HD), BF16),
        in_specs=[vmem(), vmem()],
        out_specs=vmem(),
        compiler_params=params(24),
        name="place",
    )(frm, out)


def solution(mesh):
    return jax.shard_map(
        body,
        mesh=mesh,
        in_specs=(
            P(("grp", "mlp"), None),
            P(("grp", "mlp"), None),
            P(("grp", "mlp"), None),
            P("mlp"),
            P("grp", "mlp"),
            P("grp", None),
            P(),
        ),
        out_specs=P("grp", "mlp"),
        check_vma=False,
    )
```

```python
import math

import jax
import jax.numpy as jnp
from jax import lax
from jax.experimental import pallas as pl
from jax.experimental.pallas import tpu as pltpu
from jax.sharding import PartitionSpec as P

HD = 128
HALF = 2048
IMGS = 16
BLK = 128
CHIPS = 16
CHUNKS = 2
HEADS = 8
WIDE = HEADS * HD
STEP = 4
NB = 4
ROWS = 64
CAP = 128
GROUPS = 16
GPOOL = 1024
SCALE = HD ** -0.5 / math.log(2.0)
F32 = jnp.float32
BF16 = jnp.bfloat16
I32 = jnp.int32
FIRST = (-1, 0, 1)
SECOND = (-2,)


def at(z, c):
    return (z % CHIPS) * 2 + c


def jump(k):
    return [(at(z, c), at(z + k, c)) for z in range(CHIPS) for c in range(2)]


SAME = [(at(z, 0), at(z - 1, 0)) for z in range(CHIPS)] + [(at(z, 1), at(z + 1, 1)) for z in range(CHIPS)]
OPP = [(at(z, 1), at(z - 1, 0)) for z in range(CHIPS)] + [(at(z, 0), at(z + 1, 1)) for z in range(CHIPS)]
RING = [(at(z, 0), at(z + 1, 0)) for z in range(CHIPS)] + [(at(z, 1), at(z - 1, 1)) for z in range(CHIPS)]
UP = [(at(z, c), at(z + 1, c)) for z in range(CHIPS) for c in range(2)]
DOWN = [(at(z, c), at(z - 1, c)) for z in range(CHIPS) for c in range(2)]
PART = [(at(z, c), at(z, 1 - c)) for z in range(CHIPS) for c in range(2)]


def vmem():
    return pl.BlockSpec(memory_space=pltpu.VMEM)


def smem():
    return pl.BlockSpec(memory_space=pltpu.SMEM)


def params(mib):
    return pltpu.CompilerParams(vmem_limit_bytes=mib << 20)


def cost(us):
    return pl.CostEstimate(flops=int(us * 1.15e9), bytes_accessed=int(us * 3.5e6), transcendentals=0)


def images_of(tok, grid_ref):
    image = jnp.where(tok < 0, -1, 0)
    first = jnp.zeros_like(tok)
    width = jnp.full_like(tok, grid_ref[0, 1])
    end = jnp.full_like(tok, grid_ref[0, 0] * grid_ref[0, 1])
    upto = jnp.int32(0)
    for n in range(IMGS):
        upto = upto + grid_ref[n, 0] * grid_ref[n, 1]
        past = tok >= upto
        image = jnp.where(past, n + 1, image)
        first = jnp.where(past, upto, first)
        if n + 1 < IMGS:
            width = jnp.where(past, grid_ref[n + 1, 1], width)
            end = jnp.where(past, upto + grid_ref[n + 1, 0] * grid_ref[n + 1, 1], end)
        else:
            width = jnp.where(past, 2, width)
    return image, first, width, end


def divide(a, b):
    return jnp.floor((a.astype(F32) + 0.5) / b.astype(F32)).astype(I32)


def rope_kernel(scal_ref, grid_ref, q_ref, k_ref, v_ref, own_ref, oth_ref, cos_ref, sin_ref):
    lane = lax.broadcasted_iota(I32, (BLK, HD), 1)
    low = (lane % 64) < 32
    step = pl.program_id(0)

    @pl.when(step == 0)
    def _():
        tok = scal_ref[0] * BLK + lax.broadcasted_iota(I32, (BLK, HD), 0)
        _, first, width, _ = images_of(tok, grid_ref)
        local = tok - first
        row = divide(local, width)
        col = local - row * width
        freq = jnp.exp((lane % 32).astype(F32) * (-math.log(100.0) / 32.0))
        ang = jnp.where(lane < 64, row, col).astype(F32) * freq
        cos_ref[...] = jnp.cos(ang)
        sin = jnp.sin(ang)
        sin_ref[...] = jnp.where(low, -sin, sin)

    def fill(out_ref):
        cos = cos_ref[...]
        sin = sin_ref[...]
        for h in range(STEP):
            lanes = slice(h * HD, (h + 1) * HD)
            for i, ref in ((0, q_ref), (1, k_ref)):
                x = ref[:, lanes].astype(F32)
                swap = jnp.where(low, pltpu.roll(x, 96, 1), pltpu.roll(x, 32, 1))
                out_ref[i, :, lanes] = (x * cos + swap * sin).astype(BF16)
        out_ref[2] = v_ref[...]

    n = HEADS // STEP

    @pl.when(step < n)
    def _():
        fill(oth_ref)

    @pl.when(step >= n)
    def _():
        fill(own_ref)


def rope(scal, grids, queries, keys, values, chunk):
    n = HEADS // STEP
    lanes = STEP * HD

    def src(i, scal_ref):
        half = jnp.where(i < n, 1 - scal_ref[1], scal_ref[1])
        return (0, half * (HALF // lanes) + chunk * n + i % n)

    return pl.pallas_call(
        rope_kernel,
        out_shape=[jax.ShapeDtypeStruct((3, BLK, WIDE), BF16)] * 2,
        grid_spec=pltpu.PrefetchScalarGridSpec(
            num_scalar_prefetch=1,
            grid=(2 * n,),
            in_specs=[smem()] + [pl.BlockSpec((BLK, lanes), src)] * 3,
            out_specs=[
                pl.BlockSpec((3, BLK, lanes), lambda i, _: (0, 0, jnp.maximum(i - n, 0))),
                pl.BlockSpec((3, BLK, lanes), lambda i, _: (0, 0, jnp.minimum(i, n - 1))),
            ],
            scratch_shapes=[pltpu.VMEM((BLK, HD), F32)] * 2,
        ),
        compiler_params=params(56),
        cost_estimate=cost(4),
        name="rope",
    )(scal, grids, queries, keys, values)


def layout_kernel(scal_ref, grid_ref, qhot_ref, khot_ref, pool_ref):
    chip = scal_ref[0] // 2
    core = scal_ref[1]
    lo = chip * 2 * BLK
    hi = lo + 2 * BLK
    for i in range(NB):
        tok = lo + BLK * jnp.where(core == 0, i, 1 - i) + lax.broadcasted_iota(I32, (BLK, HD), 0)
        image, _, _, _ = images_of(tok, grid_ref)
        hot = image + 1 == lax.broadcasted_iota(I32, (BLK, HD), 1)
        qhot_ref[i * BLK : (i + 1) * BLK, :] = jnp.where(hot, 256.0, 0.0).astype(BF16)
        khot_ref[i * BLK : (i + 1) * BLK, :] = jnp.where(hot, 128.0, 0.0).astype(BF16)
    lane = lax.broadcasted_iota(I32, (8, NB * BLK), 1)
    place = lane // BLK
    tok = lo + lane % BLK + BLK * jnp.where(core == 0, place, 1 - place)
    image, first, width, end = images_of(tok, grid_ref)
    local = tok - first
    prow = divide(jnp.maximum(local, 0), width)
    pcol = local - prow * width
    target = first // 4 + (prow // 2) * (width // 2) + pcol // 2
    begins = (first >= lo) & (first < hi)
    ends = (end > lo) & (end <= hi)
    owned = jnp.where(core == 0, begins.astype(I32), ends.astype(I32)) > 0
    target = jnp.where(owned & (image >= 0) & (image < IMGS), target, -1)[:1]
    r = lax.broadcasted_iota(I32, (2 * ROWS, NB * BLK), 0)
    far = jnp.where(core == 0, ROWS, -ROWS)
    mine = chip * ROWS + jnp.where(r < ROWS, r, r - ROWS + far)
    pool_ref[...] = jnp.where((target == mine) & (target >= 0), 1.0, 0.0).astype(BF16)


def attend_kernel(a_ref, b_ref, c_ref, d_ref, qhot_ref, khot_ref, pool_ref, mid_ref, edge_ref):
    refs = (a_ref, b_ref, c_ref, d_ref)
    pairs = NB // 2
    ones = jnp.ones((16, NB * BLK), BF16)
    nt = (((1,), (1,)), ((), ()))

    def score(h, i):
        lanes = slice(h * HD, (h + 1) * HD)
        keys = jnp.concatenate([ref[1, :, lanes] for ref in refs], axis=0)
        keys = jnp.concatenate([keys, khot_ref[...]], axis=1)
        q = jnp.concatenate([ref[0, :, lanes] for ref in refs[2 * i : 2 * i + 2]], axis=0)
        q = jnp.concatenate([q, qhot_ref[i * 2 * BLK : (i + 1) * 2 * BLK, :]], axis=1)
        return lax.dot_general(keys, q, nt, preferred_element_type=F32)

    def mix(h, s):
        lanes = slice(h * HD, (h + 1) * HD)
        e = jnp.exp2((s - jnp.max(s, axis=0, keepdims=True)) * SCALE).astype(BF16)
        vals = jnp.concatenate([ref[2, :, lanes] for ref in refs], axis=0)
        o = jnp.dot(jnp.concatenate([vals.T, ones], axis=0), e, preferred_element_type=F32)
        return (o[:HD] / o[HD : HD + 1]).astype(BF16)

    order = [(h, i) for h in range(STEP) for i in range(pairs)]
    later = score(*order[0])
    done = []
    for t, (h, i) in enumerate(order):
        now = later
        if t + 1 < len(order):
            later = score(*order[t + 1])
        done.append(mix(h, now))
        if len(done) == pairs:
            branch = jnp.concatenate(done, axis=1)
            done = []
            pooled = lax.dot_general(pool_ref[...], branch, nt, preferred_element_type=F32)
            pooled = (0.25 * pooled).astype(BF16)
            lanes = slice(h * HD, (h + 1) * HD)
            mid_ref[:, lanes] = pooled[:ROWS]
            edge_ref[:, lanes] = pooled[ROWS:]


def attend(parts, tables):
    part = pl.BlockSpec((3, BLK, STEP * HD), lambda h: (0, 0, h))
    whole = [pl.BlockSpec(t.shape, lambda h: (0, 0)) for t in tables]
    return pl.pallas_call(
        attend_kernel,
        grid=(HEADS // STEP,),
        out_shape=[jax.ShapeDtypeStruct((ROWS, WIDE), BF16)] * 2,
        in_specs=[part] * NB + whole,
        out_specs=[pl.BlockSpec((ROWS, STEP * HD), lambda h: (0, h))] * 2,
        compiler_params=params(56),
        cost_estimate=cost(6),
        name="attend",
    )(*parts, *tables)


def project_kernel(scal_ref, *refs):
    w_ref, got_ref, mine_ref, send_ref = refs[-4:]
    rows = jnp.concatenate([ref[...] for ref in refs[:-4]], axis=0)
    mine_ref[...] = jnp.dot(rows, w_ref[0], preferred_element_type=F32)
    send_ref[...] = jnp.dot(rows, got_ref[...], preferred_element_type=F32)


def project(scal, shards, cols, got):
    n = len(shards)
    shape = jax.ShapeDtypeStruct((n * ROWS, 4 * HD), F32)
    col = pl.BlockSpec((HALF, HD), lambda j, _: (0, j))
    out = pl.BlockSpec((n * ROWS, HD), lambda j, _: (0, j))
    return pl.pallas_call(
        project_kernel,
        out_shape=[shape] * 2,
        grid_spec=pltpu.PrefetchScalarGridSpec(
            num_scalar_prefetch=1,
            grid=(4,),
            in_specs=[pl.BlockSpec((ROWS, HALF), lambda j, _: (0, 0))] * n
            + [pl.BlockSpec((1, HALF, HD), lambda j, s: (s[1], 0, j)), col],
            out_specs=[out, out],
        ),
        compiler_params=params(24),
        cost_estimate=cost(4),
        name="project",
    )(scal, *shards, cols, got)


def join_kernel(mine_ref, got_ref, *out_refs):
    for k, ref in enumerate(out_refs):
        lanes = slice(k * HD, (k + 1) * HD)
        ref[...] = (mine_ref[:, lanes] + got_ref[:, lanes]).astype(BF16)


def join(mine, got):
    return pl.pallas_call(
        join_kernel,
        out_shape=[jax.ShapeDtypeStruct((mine.shape[0], HD), BF16)] * 4,
        in_specs=[vmem(), vmem()],
        out_specs=[vmem()] * 4,
        compiler_params=params(16),
        cost_estimate=cost(1),
        name="join",
    )(mine, got)


def index_kernel(scal_ref, pos_ref, to_ref, from_ref):
    group = scal_ref[2]
    i = lax.broadcasted_iota(I32, (GPOOL, GPOOL), 0)
    j = lax.broadcasted_iota(I32, (GPOOL, GPOOL), 1)
    before = jnp.where(i < j, 1.0, 0.0).astype(BF16)
    own = pos_ref[pl.ds(group, 1), :] // GPOOL
    hot = (own == lax.broadcasted_iota(I32, (GROUPS, GPOOL), 0)).astype(F32)
    count = jnp.dot(hot.astype(BF16), before, preferred_element_type=F32)
    rank = jnp.sum(hot * count, axis=0, keepdims=True)
    to_ref[...] = own * CAP + rank.astype(I32)
    pos = pos_ref[...]
    here = pos // GPOOL == group
    rank = jnp.dot(here.astype(F32).astype(BF16), before, preferred_element_type=F32).astype(I32)
    rank = jnp.where(here, rank, -1)
    local = pos % GPOOL + 1
    high = (local // 32).astype(F32)
    low = (local % 32).astype(F32)
    r = lax.broadcasted_iota(I32, (CAP, GPOOL), 0)
    for g in range(GROUPS):
        pick = (rank[g : g + 1] == r).astype(F32).astype(BF16)
        pair = jnp.concatenate([high[g : g + 1], low[g : g + 1], jnp.zeros((6, GPOOL), F32)], axis=0)
        got = lax.dot_general(pair.astype(BF16), pick, (((1,), (1,)), ((), ())), preferred_element_type=F32)
        value = got[0:1] * 32.0 + got[1:2] - 1.0
        from_ref[:, g * CAP : (g + 1) * CAP] = value.astype(I32)


def pack_kernel(scal_ref, to_ref, *refs):
    chip = scal_ref[0] // 2
    out_ref, all_ref = refs[-2:]
    for refs_k, shards in ((refs[:4], FIRST), (refs[4:8], SECOND)):
        for k, ref in enumerate(refs_k):
            for i, off in enumerate(shards):
                row = ((chip - 4 * k + off + 2 * CHIPS) % CHIPS) * ROWS
                all_ref[pl.ds(pl.multiple_of(row, ROWS), ROWS), :] = ref[i * ROWS : (i + 1) * ROWS, :]
    rows = 256
    for i in range(GROUPS * CAP // rows):
        r = i * rows + lax.broadcasted_iota(I32, (rows, GPOOL), 0)
        pick = jnp.where(to_ref[...] == r, 1.0, 0.0).astype(BF16)
        out_ref[i * rows : (i + 1) * rows, :] = jnp.dot(pick, all_ref[...], preferred_element_type=F32).astype(BF16)


def place_kernel(from_ref, got_ref, out_ref):
    rows = 256
    for i in range(GPOOL // rows):
        r = i * rows + lax.broadcasted_iota(I32, (rows, GROUPS * CAP), 0)
        pick = jnp.where(from_ref[...] == r, 1.0, 0.0).astype(BF16)
        out_ref[i * rows : (i + 1) * rows, :] = jnp.dot(pick, got_ref[...], preferred_element_type=F32).astype(BF16)


def body(queries, keys, values, gamma, w_merge, grids, positions):
    me = lax.axis_index("mlp")
    core = me % 2
    scal = jnp.stack([me, core, lax.axis_index("grp"), me]).astype(I32)
    shape = jax.ShapeDtypeStruct

    def move(x, perm):
        return lax.ppermute(x, "mlp", perm)

    cols = jnp.concatenate([w_merge] + [move(w_merge, jump(-4 * k)) for k in (1, 2, 3)], axis=1)
    cols = lax.all_gather(cols, "grp", axis=0, tiled=True).reshape(2, HALF, 4 * HD)

    parts = []
    for chunk in range(CHUNKS):
        own, oth = rope(scal, grids, queries, keys, values, chunk)
        parts.append([own, move(oth, PART), move(own, SAME), move(oth, OPP)])

    tables = pl.pallas_call(
        layout_kernel,
        out_shape=[shape((NB * BLK, HD), BF16)] * 2 + [shape((2 * ROWS, NB * BLK), BF16)],
        in_specs=[smem(), smem()],
        out_specs=[vmem()] * 3,
        compiler_params=params(16),
        name="layout",
    )(scal, grids)
    to, frm = pl.pallas_call(
        index_kernel,
        out_shape=[shape((1, GPOOL), I32), shape((1, GROUPS * CAP), I32)],
        in_specs=[smem(), vmem()],
        out_specs=[vmem(), vmem()],
        compiler_params=params(24),
        name="index",
    )(scal, positions.reshape(GROUPS, GPOOL))
    owns, tables, to, frm = lax.optimization_barrier(([p[0] for p in parts], tables, to, frm))
    gains = jnp.broadcast_to(gamma[None, :], (2 * CHIPS, HD))
    pooled = []
    for chunk in range(CHUNKS):
        mid, edge = attend([owns[chunk]] + parts[chunk][1:], tables)
        edge = move(edge, RING)
        pooled.append((mid, edge))
        if chunk == 0:
            gains, _ = lax.optimization_barrier((gains, mid))
            gains = lax.all_to_all(gains, "mlp", split_axis=0, concat_axis=0, tiled=True)
            gains = lax.dynamic_slice_in_dim(gains, core * CHIPS, CHIPS, 0).reshape(1, HALF).astype(F32)
        tables, _ = lax.optimization_barrier((tables, edge))
    rows = jnp.concatenate([mid + edge for mid, edge in pooled], axis=1)
    rows = (rows.astype(F32) * gains).astype(BF16)
    below = move(rows, UP)
    above = move(rows, DOWN)
    last = move(below, UP)
    cols, _ = lax.optimization_barrier((cols, (below, above)))
    cols_got = move(lax.dynamic_index_in_dim(cols, 1 - core, 0, keepdims=False), PART)

    pieces = []
    for shards in ((below, rows, above), (last,)):
        mine, send = project(scal, shards, cols, cols_got)
        blocks = join(mine, move(send, PART))
        pieces += [blocks[0]] + [move(blocks[k], jump(4 * k)) for k in (1, 2, 3)]

    out = pl.pallas_call(
        pack_kernel,
        out_shape=shape((GROUPS * CAP, HD), BF16),
        in_specs=[smem()] + [vmem()] * (1 + len(pieces)),
        out_specs=vmem(),
        scratch_shapes=[pltpu.VMEM((GPOOL, HD), BF16)],
        compiler_params=params(24),
        name="pack",
    )(scal, to, *pieces)
    out = lax.all_to_all(out, "grp", split_axis=0, concat_axis=0, tiled=True)
    return pl.pallas_call(
        place_kernel,
        out_shape=shape((GPOOL, HD), BF16),
        in_specs=[vmem(), vmem()],
        out_specs=vmem(),
        compiler_params=params(24),
        name="place",
    )(frm, out)


def solution(mesh):
    return jax.shard_map(
        body,
        mesh=mesh,
        in_specs=(
            P(("grp", "mlp"), None),
            P(("grp", "mlp"), None),
            P(("grp", "mlp"), None),
            P("mlp"),
            P("grp", "mlp"),
            P("grp", None),
            P(),
        ),
        out_specs=P("grp", "mlp"),
        check_vma=False,
    )
```

```python
import math

import jax
import jax.numpy as jnp
from jax import lax
from jax.experimental import pallas as pl
from jax.experimental.pallas import tpu as pltpu
from jax.sharding import PartitionSpec as P

HD = 128
HALF = 2048
IMGS = 16
BLK = 128
CHIPS = 16
CHUNKS = 2
HEADS = 8
WIDE = HEADS * HD
STEP = 4
NB = 4
ROWS = 64
CAP = 128
GROUPS = 16
GPOOL = 1024
SCALE = HD ** -0.5 / math.log(2.0)
F32 = jnp.float32
BF16 = jnp.bfloat16
I32 = jnp.int32
WINDOW = (-1, 0, 1, -2)
QUADS = 4


def at(z, c):
    return (z % CHIPS) * 2 + c


SAME = [(at(z, 0), at(z - 1, 0)) for z in range(CHIPS)] + [(at(z, 1), at(z + 1, 1)) for z in range(CHIPS)]
OPP = [(at(z, 1), at(z - 1, 0)) for z in range(CHIPS)] + [(at(z, 0), at(z + 1, 1)) for z in range(CHIPS)]
RING = [(at(z, 0), at(z + 1, 0)) for z in range(CHIPS)] + [(at(z, 1), at(z - 1, 1)) for z in range(CHIPS)]
UP = [(at(z, c), at(z + 1, c)) for z in range(CHIPS) for c in range(2)]
DOWN = [(at(z, c), at(z - 1, c)) for z in range(CHIPS) for c in range(2)]
FOURS = [[at(r + QUADS * k, c) for k in range(QUADS)] for r in range(QUADS) for c in range(2)]
PART = [(at(z, c), at(z, 1 - c)) for z in range(CHIPS) for c in range(2)]


def vmem():
    return pl.BlockSpec(memory_space=pltpu.VMEM)


def smem():
    return pl.BlockSpec(memory_space=pltpu.SMEM)


def params(mib):
    return pltpu.CompilerParams(vmem_limit_bytes=mib << 20)


def cost(us):
    return pl.CostEstimate(flops=int(us * 1.15e9), bytes_accessed=int(us * 3.5e6), transcendentals=0)


def images_of(tok, grid_ref):
    image = jnp.where(tok < 0, -1, 0)
    first = jnp.zeros_like(tok)
    width = jnp.full_like(tok, grid_ref[0, 1])
    end = jnp.full_like(tok, grid_ref[0, 0] * grid_ref[0, 1])
    upto = jnp.int32(0)
    for n in range(IMGS):
        upto = upto + grid_ref[n, 0] * grid_ref[n, 1]
        past = tok >= upto
        image = jnp.where(past, n + 1, image)
        first = jnp.where(past, upto, first)
        if n + 1 < IMGS:
            width = jnp.where(past, grid_ref[n + 1, 1], width)
            end = jnp.where(past, upto + grid_ref[n + 1, 0] * grid_ref[n + 1, 1], end)
        else:
            width = jnp.where(past, 2, width)
    return image, first, width, end


def divide(a, b):
    return jnp.floor((a.astype(F32) + 0.5) / b.astype(F32)).astype(I32)


def rope_kernel(scal_ref, grid_ref, q_ref, k_ref, v_ref, own_ref, oth_ref, cos_ref, sin_ref):
    lane = lax.broadcasted_iota(I32, (BLK, HD), 1)
    low = (lane % 64) < 32
    step = pl.program_id(0)

    @pl.when(step == 0)
    def _():
        tok = scal_ref[0] * BLK + lax.broadcasted_iota(I32, (BLK, HD), 0)
        _, first, width, _ = images_of(tok, grid_ref)
        local = tok - first
        row = divide(local, width)
        col = local - row * width
        freq = jnp.exp((lane % 32).astype(F32) * (-math.log(100.0) / 32.0))
        ang = jnp.where(lane < 64, row, col).astype(F32) * freq
        cos_ref[...] = jnp.cos(ang)
        sin = jnp.sin(ang)
        sin_ref[...] = jnp.where(low, -sin, sin)

    def fill(out_ref):
        cos = cos_ref[...]
        sin = sin_ref[...]
        for h in range(STEP):
            lanes = slice(h * HD, (h + 1) * HD)
            for i, ref in ((0, q_ref), (1, k_ref)):
                x = ref[:, lanes].astype(F32)
                swap = jnp.where(low, pltpu.roll(x, 96, 1), pltpu.roll(x, 32, 1))
                out_ref[i, :, lanes] = (x * cos + swap * sin).astype(BF16)
        out_ref[2] = v_ref[...]

    n = HEADS // STEP

    @pl.when(step < n)
    def _():
        fill(oth_ref)

    @pl.when(step >= n)
    def _():
        fill(own_ref)


def rope(scal, grids, queries, keys, values, chunk):
    n = HEADS // STEP
    lanes = STEP * HD

    def src(i, scal_ref):
        half = jnp.where(i < n, 1 - scal_ref[1], scal_ref[1])
        return (0, half * (HALF // lanes) + chunk * n + i % n)

    return pl.pallas_call(
        rope_kernel,
        out_shape=[jax.ShapeDtypeStruct((3, BLK, WIDE), BF16)] * 2,
        grid_spec=pltpu.PrefetchScalarGridSpec(
            num_scalar_prefetch=1,
            grid=(2 * n,),
            in_specs=[smem()] + [pl.BlockSpec((BLK, lanes), src)] * 3,
            out_specs=[
                pl.BlockSpec((3, BLK, lanes), lambda i, _: (0, 0, jnp.maximum(i - n, 0))),
                pl.BlockSpec((3, BLK, lanes), lambda i, _: (0, 0, jnp.minimum(i, n - 1))),
            ],
            scratch_shapes=[pltpu.VMEM((BLK, HD), F32)] * 2,
        ),
        compiler_params=params(56),
        cost_estimate=cost(4),
        name="rope",
    )(scal, grids, queries, keys, values)


def layout_kernel(scal_ref, grid_ref, qhot_ref, khot_ref, pool_ref):
    chip = scal_ref[0] // 2
    core = scal_ref[1]
    lo = chip * 2 * BLK
    hi = lo + 2 * BLK
    for i in range(NB):
        tok = lo + BLK * jnp.where(core == 0, i, 1 - i) + lax.broadcasted_iota(I32, (BLK, HD), 0)
        image, _, _, _ = images_of(tok, grid_ref)
        hot = image + 1 == lax.broadcasted_iota(I32, (BLK, HD), 1)
        qhot_ref[i * BLK : (i + 1) * BLK, :] = jnp.where(hot, 256.0, 0.0).astype(BF16)
        khot_ref[i * BLK : (i + 1) * BLK, :] = jnp.where(hot, 128.0, 0.0).astype(BF16)
    lane = lax.broadcasted_iota(I32, (8, NB * BLK), 1)
    place = lane // BLK
    tok = lo + lane % BLK + BLK * jnp.where(core == 0, place, 1 - place)
    image, first, width, end = images_of(tok, grid_ref)
    local = tok - first
    prow = divide(jnp.maximum(local, 0), width)
    pcol = local - prow * width
    target = first // 4 + (prow // 2) * (width // 2) + pcol // 2
    begins = (first >= lo) & (first < hi)
    ends = (end > lo) & (end <= hi)
    owned = jnp.where(core == 0, begins.astype(I32), ends.astype(I32)) > 0
    target = jnp.where(owned & (image >= 0) & (image < IMGS), target, -1)[:1]
    r = lax.broadcasted_iota(I32, (2 * ROWS, NB * BLK), 0)
    far = jnp.where(core == 0, ROWS, -ROWS)
    mine = chip * ROWS + jnp.where(r < ROWS, r, r - ROWS + far)
    pool_ref[...] = jnp.where((target == mine) & (target >= 0), 1.0, 0.0).astype(BF16)


def attend_kernel(a_ref, b_ref, c_ref, d_ref, qhot_ref, khot_ref, pool_ref, mid_ref, edge_ref):
    refs = (a_ref, b_ref, c_ref, d_ref)
    pairs = NB // 2
    ones = jnp.ones((16, NB * BLK), BF16)
    nt = (((1,), (1,)), ((), ()))

    def score(h, i):
        lanes = slice(h * HD, (h + 1) * HD)
        keys = jnp.concatenate([ref[1, :, lanes] for ref in refs], axis=0)
        keys = jnp.concatenate([keys, khot_ref[...]], axis=1)
        q = jnp.concatenate([ref[0, :, lanes] for ref in refs[2 * i : 2 * i + 2]], axis=0)
        q = jnp.concatenate([q, qhot_ref[i * 2 * BLK : (i + 1) * 2 * BLK, :]], axis=1)
        return lax.dot_general(keys, q, nt, preferred_element_type=F32)

    def mix(h, s):
        lanes = slice(h * HD, (h + 1) * HD)
        e = jnp.exp2((s - jnp.max(s, axis=0, keepdims=True)) * SCALE).astype(BF16)
        vals = jnp.concatenate([ref[2, :, lanes] for ref in refs], axis=0)
        o = jnp.dot(jnp.concatenate([vals.T, ones], axis=0), e, preferred_element_type=F32)
        return (o[:HD] / o[HD : HD + 1]).astype(BF16)

    order = [(h, i) for h in range(STEP) for i in range(pairs)]
    later = score(*order[0])
    done = []
    for t, (h, i) in enumerate(order):
        now = later
        if t + 1 < len(order):
            later = score(*order[t + 1])
        done.append(mix(h, now))
        if len(done) == pairs:
            branch = jnp.concatenate(done, axis=1)
            done = []
            pooled = lax.dot_general(pool_ref[...], branch, nt, preferred_element_type=F32)
            pooled = (0.25 * pooled).astype(BF16)
            lanes = slice(h * HD, (h + 1) * HD)
            mid_ref[:, lanes] = pooled[:ROWS]
            edge_ref[:, lanes] = pooled[ROWS:]


def attend(parts, tables):
    part = pl.BlockSpec((3, BLK, STEP * HD), lambda h: (0, 0, h))
    whole = [pl.BlockSpec(t.shape, lambda h: (0, 0)) for t in tables]
    return pl.pallas_call(
        attend_kernel,
        grid=(HEADS // STEP,),
        out_shape=[jax.ShapeDtypeStruct((ROWS, WIDE), BF16)] * 2,
        in_specs=[part] * NB + whole,
        out_specs=[pl.BlockSpec((ROWS, STEP * HD), lambda h: (0, h))] * 2,
        compiler_params=params(56),
        cost_estimate=cost(6),
        name="attend",
    )(*parts, *tables)


def project_kernel(scal_ref, *refs):
    w_own_ref, w_oth_ref, out_ref = refs[-3:]
    own = jnp.concatenate([ref[...] for ref in refs[:NB]], axis=0)
    oth = jnp.concatenate([ref[...] for ref in refs[NB : 2 * NB]], axis=0)
    total = jnp.dot(own, w_own_ref[...].reshape(HALF, HD), preferred_element_type=F32)
    total += jnp.dot(oth, w_oth_ref[...].reshape(HALF, HD), preferred_element_type=F32)
    out_ref[0] = total.astype(BF16)


def project(scal, own, oth, cols):
    rows = NB * ROWS
    half = (GROUPS // 2, 1, 2 * BLK, HD)
    return pl.pallas_call(
        project_kernel,
        out_shape=jax.ShapeDtypeStruct((QUADS, rows, HD), BF16),
        grid_spec=pltpu.PrefetchScalarGridSpec(
            num_scalar_prefetch=1,
            grid=(QUADS,),
            in_specs=[pl.BlockSpec((ROWS, HALF), lambda j, _: (0, 0))] * (2 * NB)
            + [
                pl.BlockSpec(half, lambda j, s: (s[1], j, 0, 0)),
                pl.BlockSpec(half, lambda j, s: (1 - s[1], j, 0, 0)),
            ],
            out_specs=pl.BlockSpec((1, rows, HD), lambda j, _: (j, 0, 0)),
        ),
        compiler_params=params(24),
        cost_estimate=cost(4),
        name="project",
    )(scal, *own, *oth, cols, cols)


def index_kernel(scal_ref, pos_ref, to_ref, from_ref):
    group = scal_ref[2]
    i = lax.broadcasted_iota(I32, (GPOOL, GPOOL), 0)
    j = lax.broadcasted_iota(I32, (GPOOL, GPOOL), 1)
    before = jnp.where(i < j, 1.0, 0.0).astype(BF16)
    own = pos_ref[pl.ds(group, 1), :] // GPOOL
    hot = (own == lax.broadcasted_iota(I32, (GROUPS, GPOOL), 0)).astype(F32)
    count = jnp.dot(hot.astype(BF16), before, preferred_element_type=F32)
    rank = jnp.sum(hot * count, axis=0, keepdims=True)
    to_ref[...] = own * CAP + rank.astype(I32)
    pos = pos_ref[...]
    here = pos // GPOOL == group
    rank = jnp.dot(here.astype(F32).astype(BF16), before, preferred_element_type=F32).astype(I32)
    rank = jnp.where(here, rank, -1)
    local = pos % GPOOL + 1
    high = (local // 32).astype(F32)
    low = (local % 32).astype(F32)
    r = lax.broadcasted_iota(I32, (CAP, GPOOL), 0)
    for g in range(GROUPS):
        pick = (rank[g : g + 1] == r).astype(F32).astype(BF16)
        pair = jnp.concatenate([high[g : g + 1], low[g : g + 1], jnp.zeros((6, GPOOL), F32)], axis=0)
        got = lax.dot_general(pair.astype(BF16), pick, (((1,), (1,)), ((), ())), preferred_element_type=F32)
        value = got[0:1] * 32.0 + got[1:2] - 1.0
        from_ref[:, g * CAP : (g + 1) * CAP] = value.astype(I32)


def pack_kernel(scal_ref, to_ref, got_ref, out_ref, all_ref):
    chip = scal_ref[0] // 2
    for k in range(QUADS):
        source = chip % QUADS + QUADS * k
        for i, off in enumerate(WINDOW):
            row = ((source + off + CHIPS) % CHIPS) * ROWS
            all_ref[pl.ds(pl.multiple_of(row, ROWS), ROWS), :] = got_ref[k, i * ROWS : (i + 1) * ROWS, :]
    rows = 256
    for i in range(GROUPS * CAP // rows):
        r = i * rows + lax.broadcasted_iota(I32, (rows, GPOOL), 0)
        pick = jnp.where(to_ref[...] == r, 1.0, 0.0).astype(BF16)
        out_ref[i * rows : (i + 1) * rows, :] = jnp.dot(pick, all_ref[...], preferred_element_type=F32).astype(BF16)


def place_kernel(from_ref, got_ref, out_ref):
    rows = 256
    for i in range(GPOOL // rows):
        r = i * rows + lax.broadcasted_iota(I32, (rows, GROUPS * CAP), 0)
        pick = jnp.where(from_ref[...] == r, 1.0, 0.0).astype(BF16)
        out_ref[i * rows : (i + 1) * rows, :] = jnp.dot(pick, got_ref[...], preferred_element_type=F32).astype(BF16)


def body(queries, keys, values, gamma, w_merge, grids, positions):
    me = lax.axis_index("mlp")
    core = me % 2
    scal = jnp.stack([me, core, lax.axis_index("grp"), me]).astype(I32)
    shape = jax.ShapeDtypeStruct

    def move(x, perm):
        return lax.ppermute(x, "mlp", perm)

    cols = lax.all_gather(w_merge, "mlp", axis=0, axis_index_groups=FOURS)
    cols = lax.all_gather(cols, "grp", axis=0)

    parts = []
    for chunk in range(CHUNKS):
        own, oth = rope(scal, grids, queries, keys, values, chunk)
        parts.append([own, move(oth, PART), move(own, SAME), move(oth, OPP)])

    tables = pl.pallas_call(
        layout_kernel,
        out_shape=[shape((NB * BLK, HD), BF16)] * 2 + [shape((2 * ROWS, NB * BLK), BF16)],
        in_specs=[smem(), smem()],
        out_specs=[vmem()] * 3,
        compiler_params=params(16),
        name="layout",
    )(scal, grids)
    to, frm = pl.pallas_call(
        index_kernel,
        out_shape=[shape((1, GPOOL), I32), shape((1, GROUPS * CAP), I32)],
        in_specs=[smem(), vmem()],
        out_specs=[vmem(), vmem()],
        compiler_params=params(24),
        name="index",
    )(scal, positions.reshape(GROUPS, GPOOL))
    owns, tables, to, frm = lax.optimization_barrier(([p[0] for p in parts], tables, to, frm))
    gains = jnp.broadcast_to(gamma[None, :], (2 * CHIPS, HD))
    pooled = []
    for chunk in range(CHUNKS):
        mid, edge = attend([owns[chunk]] + parts[chunk][1:], tables)
        edge = move(edge, RING)
        pooled.append((mid, edge))
        if chunk == 0:
            gains, _ = lax.optimization_barrier((gains, mid))
            gains = lax.all_to_all(gains, "mlp", split_axis=0, concat_axis=0, tiled=True)
            gains = lax.dynamic_slice_in_dim(gains, core * CHIPS, CHIPS, 0).reshape(1, HALF).astype(F32)
        tables, _ = lax.optimization_barrier((tables, edge))
    rows = jnp.concatenate([mid + edge for mid, edge in pooled], axis=1)
    rows = (rows.astype(F32) * gains).astype(BF16)
    below = move(rows, UP)
    above = move(rows, DOWN)
    last = move(below, UP)
    own = (below, rows, above, last)
    oth = [move(x, PART) for x in own]
    cols, _ = lax.optimization_barrier((cols, (below, above)))
    out = project(scal, own, oth, cols)
    out = lax.all_to_all(out, "mlp", split_axis=0, concat_axis=0, tiled=True, axis_index_groups=FOURS)

    out = pl.pallas_call(
        pack_kernel,
        out_shape=shape((GROUPS * CAP, HD), BF16),
        in_specs=[smem(), vmem(), vmem()],
        out_specs=vmem(),
        scratch_shapes=[pltpu.VMEM((GPOOL, HD), BF16)],
        compiler_params=params(24),
        name="pack",
    )(scal, to, out)
    out = lax.all_to_all(out, "grp", split_axis=0, concat_axis=0, tiled=True)
    return pl.pallas_call(
        place_kernel,
        out_shape=shape((GPOOL, HD), BF16),
        in_specs=[vmem(), vmem()],
        out_specs=vmem(),
        compiler_params=params(24),
        name="place",
    )(frm, out)


def solution(mesh):
    return jax.shard_map(
        body,
        mesh=mesh,
        in_specs=(
            P(("grp", "mlp"), None),
            P(("grp", "mlp"), None),
            P(("grp", "mlp"), None),
            P("mlp"),
            P("grp", "mlp"),
            P("grp", None),
            P(),
        ),
        out_specs=P("grp", "mlp"),
        check_vma=False,
    )
```

```python
import math

import jax
import jax.numpy as jnp
from jax import lax
from jax.experimental import pallas as pl
from jax.experimental.pallas import tpu as pltpu
from jax.sharding import Mesh
from jax.sharding import PartitionSpec as P

HD = 128
HALF = 2048
IMGS = 16
BLK = 128
CHIPS = 16
CHUNKS = 2
HEADS = 8
WIDE = HEADS * HD
STEP = 4
NB = 4
ROWS = 64
CAP = 128
GROUPS = 16
GPOOL = 1024
SCALE = HD ** -0.5 / math.log(2.0)
F32 = jnp.float32
BF16 = jnp.bfloat16
I32 = jnp.int32
MLP = ("zq", "zr", "core")
WINDOW = (-1, 0, 1, -2)
QUADS = 4


def at(z, c):
    return (z % CHIPS) * 2 + c


SAME = [(at(z, 0), at(z - 1, 0)) for z in range(CHIPS)] + [(at(z, 1), at(z + 1, 1)) for z in range(CHIPS)]
OPP = [(at(z, 1), at(z - 1, 0)) for z in range(CHIPS)] + [(at(z, 0), at(z + 1, 1)) for z in range(CHIPS)]
RING = [(at(z, 0), at(z + 1, 0)) for z in range(CHIPS)] + [(at(z, 1), at(z - 1, 1)) for z in range(CHIPS)]
UP = [(at(z, c), at(z + 1, c)) for z in range(CHIPS) for c in range(2)]
DOWN = [(at(z, c), at(z - 1, c)) for z in range(CHIPS) for c in range(2)]
PART = [(at(z, c), at(z, 1 - c)) for z in range(CHIPS) for c in range(2)]


def vmem():
    return pl.BlockSpec(memory_space=pltpu.VMEM)


def smem():
    return pl.BlockSpec(memory_space=pltpu.SMEM)


def params(mib):
    return pltpu.CompilerParams(vmem_limit_bytes=mib << 20)


def cost(us):
    return pl.CostEstimate(flops=int(us * 1.15e9), bytes_accessed=int(us * 3.5e6), transcendentals=0)


def images_of(tok, grid_ref):
    image = jnp.where(tok < 0, -1, 0)
    first = jnp.zeros_like(tok)
    width = jnp.full_like(tok, grid_ref[0, 1])
    end = jnp.full_like(tok, grid_ref[0, 0] * grid_ref[0, 1])
    upto = jnp.int32(0)
    for n in range(IMGS):
        upto = upto + grid_ref[n, 0] * grid_ref[n, 1]
        past = tok >= upto
        image = jnp.where(past, n + 1, image)
        first = jnp.where(past, upto, first)
        if n + 1 < IMGS:
            width = jnp.where(past, grid_ref[n + 1, 1], width)
            end = jnp.where(past, upto + grid_ref[n + 1, 0] * grid_ref[n + 1, 1], end)
        else:
            width = jnp.where(past, 2, width)
    return image, first, width, end


def divide(a, b):
    return jnp.floor((a.astype(F32) + 0.5) / b.astype(F32)).astype(I32)


def rope_kernel(scal_ref, grid_ref, q_ref, k_ref, v_ref, own_ref, oth_ref, cos_ref, sin_ref):
    lane = lax.broadcasted_iota(I32, (BLK, HD), 1)
    low = (lane % 64) < 32
    step = pl.program_id(0)

    @pl.when(step == 0)
    def _():
        tok = scal_ref[0] * BLK + lax.broadcasted_iota(I32, (BLK, HD), 0)
        _, first, width, _ = images_of(tok, grid_ref)
        local = tok - first
        row = divide(local, width)
        col = local - row * width
        freq = jnp.exp((lane % 32).astype(F32) * (-math.log(100.0) / 32.0))
        ang = jnp.where(lane < 64, row, col).astype(F32) * freq
        cos_ref[...] = jnp.cos(ang)
        sin = jnp.sin(ang)
        sin_ref[...] = jnp.where(low, -sin, sin)

    def fill(out_ref):
        cos = cos_ref[...]
        sin = sin_ref[...]
        for h in range(STEP):
            lanes = slice(h * HD, (h + 1) * HD)
            for i, ref in ((0, q_ref), (1, k_ref)):
                x = ref[:, lanes].astype(F32)
                swap = jnp.where(low, pltpu.roll(x, 96, 1), pltpu.roll(x, 32, 1))
                out_ref[i, :, lanes] = (x * cos + swap * sin).astype(BF16)
        out_ref[2] = v_ref[...]

    n = HEADS // STEP

    @pl.when(step < n)
    def _():
        fill(oth_ref)

    @pl.when(step >= n)
    def _():
        fill(own_ref)


def rope(scal, grids, queries, keys, values, chunk):
    n = HEADS // STEP
    lanes = STEP * HD
    queries, keys, values = (pltpu.with_memory_space_constraint(x, pltpu.HBM) for x in (queries, keys, values))

    def src(i, scal_ref):
        half = jnp.where(i < n, 1 - scal_ref[1], scal_ref[1])
        return (0, half * (HALF // lanes) + chunk * n + i % n)

    return pl.pallas_call(
        rope_kernel,
        out_shape=[jax.ShapeDtypeStruct((3, BLK, WIDE), BF16)] * 2,
        grid_spec=pltpu.PrefetchScalarGridSpec(
            num_scalar_prefetch=1,
            grid=(2 * n,),
            in_specs=[smem()] + [pl.BlockSpec((BLK, lanes), src)] * 3,
            out_specs=[
                pl.BlockSpec((3, BLK, lanes), lambda i, _: (0, 0, jnp.maximum(i - n, 0))),
                pl.BlockSpec((3, BLK, lanes), lambda i, _: (0, 0, jnp.minimum(i, n - 1))),
            ],
            scratch_shapes=[pltpu.VMEM((BLK, HD), F32)] * 2,
        ),
        compiler_params=params(16),
        cost_estimate=cost(4),
        name="rope",
    )(scal, grids, queries, keys, values)


def layout_kernel(scal_ref, grid_ref, qhot_ref, khot_ref, pool_ref):
    chip = scal_ref[0] // 2
    core = scal_ref[1]
    lo = chip * 2 * BLK
    hi = lo + 2 * BLK
    for i in range(NB):
        tok = lo + BLK * jnp.where(core == 0, i, 1 - i) + lax.broadcasted_iota(I32, (BLK, HD), 0)
        image, _, _, _ = images_of(tok, grid_ref)
        hot = image + 1 == lax.broadcasted_iota(I32, (BLK, HD), 1)
        qhot_ref[i * BLK : (i + 1) * BLK, :] = jnp.where(hot, 256.0, 0.0).astype(BF16)
        khot_ref[i * BLK : (i + 1) * BLK, :] = jnp.where(hot, 128.0, 0.0).astype(BF16)
    lane = lax.broadcasted_iota(I32, (8, NB * BLK), 1)
    place = lane // BLK
    tok = lo + lane % BLK + BLK * jnp.where(core == 0, place, 1 - place)
    image, first, width, end = images_of(tok, grid_ref)
    local = tok - first
    prow = divide(jnp.maximum(local, 0), width)
    pcol = local - prow * width
    target = first // 4 + (prow // 2) * (width // 2) + pcol // 2
    begins = (first >= lo) & (first < hi)
    ends = (end > lo) & (end <= hi)
    owned = jnp.where(core == 0, begins.astype(I32), ends.astype(I32)) > 0
    target = jnp.where(owned & (image >= 0) & (image < IMGS), target, -1)[:1]
    r = lax.broadcasted_iota(I32, (2 * ROWS, NB * BLK), 0)
    far = jnp.where(core == 0, ROWS, -ROWS)
    mine = chip * ROWS + jnp.where(r < ROWS, r, r - ROWS + far)
    pool_ref[...] = jnp.where((target == mine) & (target >= 0), 1.0, 0.0).astype(BF16)


def attend_kernel(a_ref, b_ref, c_ref, d_ref, qhot_ref, khot_ref, pool_ref, mid_ref, edge_ref):
    refs = (a_ref, b_ref, c_ref, d_ref)
    pairs = NB // 2
    ones = jnp.ones((16, NB * BLK), BF16)
    nt = (((1,), (1,)), ((), ()))

    def score(h, i):
        lanes = slice(h * HD, (h + 1) * HD)
        keys = jnp.concatenate([ref[1, :, lanes] for ref in refs], axis=0)
        keys = jnp.concatenate([keys, khot_ref[...]], axis=1)
        q = jnp.concatenate([ref[0, :, lanes] for ref in refs[2 * i : 2 * i + 2]], axis=0)
        q = jnp.concatenate([q, qhot_ref[i * 2 * BLK : (i + 1) * 2 * BLK, :]], axis=1)
        return lax.dot_general(keys, q, nt, preferred_element_type=F32)

    def mix(h, s):
        lanes = slice(h * HD, (h + 1) * HD)
        e = jnp.exp2((s - jnp.max(s, axis=0, keepdims=True)) * SCALE).astype(BF16)
        vals = jnp.concatenate([ref[2, :, lanes] for ref in refs], axis=0)
        o = jnp.dot(jnp.concatenate([vals.T, ones], axis=0), e, preferred_element_type=F32)
        return (o[:HD] / o[HD : HD + 1]).astype(BF16)

    order = [(h, i) for h in range(STEP) for i in range(pairs)]
    later = score(*order[0])
    done = []
    for t, (h, i) in enumerate(order):
        now = later
        if t + 1 < len(order):
            later = score(*order[t + 1])
        done.append(mix(h, now))
        if len(done) == pairs:
            branch = jnp.concatenate(done, axis=1)
            done = []
            pooled = lax.dot_general(pool_ref[...], branch, nt, preferred_element_type=F32)
            pooled = (0.25 * pooled).astype(BF16)
            lanes = slice(h * HD, (h + 1) * HD)
            mid_ref[:, lanes] = pooled[:ROWS]
            edge_ref[:, lanes] = pooled[ROWS:]


def attend(parts, tables):
    part = pl.BlockSpec((3, BLK, STEP * HD), lambda h: (0, 0, h))
    whole = [pl.BlockSpec(t.shape, lambda h: (0, 0)) for t in tables]
    return pl.pallas_call(
        attend_kernel,
        grid=(HEADS // STEP,),
        out_shape=[jax.ShapeDtypeStruct((ROWS, WIDE), BF16)] * 2,
        in_specs=[part] * NB + whole,
        out_specs=[pl.BlockSpec((ROWS, STEP * HD), lambda h: (0, h))] * 2,
        compiler_params=params(32),
        cost_estimate=cost(6),
        name="attend",
    )(*parts, *tables)


def project_kernel(scal_ref, *refs):
    w_own_ref, w_oth_ref, out_ref = refs[-3:]
    own = jnp.concatenate([ref[...] for ref in refs[:NB]], axis=0)
    oth = jnp.concatenate([ref[...] for ref in refs[NB : 2 * NB]], axis=0)
    total = jnp.dot(own, w_own_ref[...].reshape(HALF, HD), preferred_element_type=F32)
    total += jnp.dot(oth, w_oth_ref[...].reshape(HALF, HD), preferred_element_type=F32)
    out_ref[0] = total.astype(BF16)


def project(scal, own, oth, cols):
    rows = NB * ROWS
    half = (GROUPS // 2, 1, 2 * BLK, HD)
    cols = pltpu.with_memory_space_constraint(cols, pltpu.HBM)
    return pl.pallas_call(
        project_kernel,
        out_shape=jax.ShapeDtypeStruct((QUADS, rows, HD), BF16),
        grid_spec=pltpu.PrefetchScalarGridSpec(
            num_scalar_prefetch=1,
            grid=(QUADS,),
            in_specs=[pl.BlockSpec((ROWS, HALF), lambda j, _: (0, 0))] * (2 * NB)
            + [
                pl.BlockSpec(half, lambda j, s: (s[1], j, 0, 0)),
                pl.BlockSpec(half, lambda j, s: (1 - s[1], j, 0, 0)),
            ],
            out_specs=pl.BlockSpec((1, rows, HD), lambda j, _: (j, 0, 0)),
        ),
        compiler_params=params(24),
        cost_estimate=cost(4),
        name="project",
    )(scal, *own, *oth, cols, cols)


def index_kernel(scal_ref, pos_ref, to_ref, from_ref):
    group = scal_ref[2]
    i = lax.broadcasted_iota(I32, (GPOOL, GPOOL), 0)
    j = lax.broadcasted_iota(I32, (GPOOL, GPOOL), 1)
    before = jnp.where(i < j, 1.0, 0.0).astype(BF16)
    own = pos_ref[pl.ds(group, 1), :] // GPOOL
    hot = (own == lax.broadcasted_iota(I32, (GROUPS, GPOOL), 0)).astype(F32)
    count = jnp.dot(hot.astype(BF16), before, preferred_element_type=F32)
    rank = jnp.sum(hot * count, axis=0, keepdims=True)
    to_ref[...] = own * CAP + rank.astype(I32)
    pos = pos_ref[...]
    here = pos // GPOOL == group
    rank = jnp.dot(here.astype(F32).astype(BF16), before, preferred_element_type=F32).astype(I32)
    rank = jnp.where(here, rank, -1)
    local = pos % GPOOL + 1
    high = (local // 32).astype(F32)
    low = (local % 32).astype(F32)
    r = lax.broadcasted_iota(I32, (CAP, GPOOL), 0)
    for g in range(GROUPS):
        pick = (rank[g : g + 1] == r).astype(F32).astype(BF16)
        pair = jnp.concatenate([high[g : g + 1], low[g : g + 1], jnp.zeros((6, GPOOL), F32)], axis=0)
        got = lax.dot_general(pair.astype(BF16), pick, (((1,), (1,)), ((), ())), preferred_element_type=F32)
        value = got[0:1] * 32.0 + got[1:2] - 1.0
        from_ref[:, g * CAP : (g + 1) * CAP] = value.astype(I32)


def pack_kernel(scal_ref, to_ref, got_ref, out_ref, all_ref):
    chip = scal_ref[0] // 2
    for k in range(QUADS):
        source = chip % QUADS + QUADS * k
        for i, off in enumerate(WINDOW):
            row = ((source + off + CHIPS) % CHIPS) * ROWS
            all_ref[pl.ds(pl.multiple_of(row, ROWS), ROWS), :] = got_ref[k, i * ROWS : (i + 1) * ROWS, :]
    rows = 256
    for i in range(GROUPS * CAP // rows):
        r = i * rows + lax.broadcasted_iota(I32, (rows, GPOOL), 0)
        pick = jnp.where(to_ref[...] == r, 1.0, 0.0).astype(BF16)
        out_ref[i * rows : (i + 1) * rows, :] = jnp.dot(pick, all_ref[...], preferred_element_type=F32).astype(BF16)


def place_kernel(from_ref, got_ref, out_ref):
    rows = 256
    for i in range(GPOOL // rows):
        r = i * rows + lax.broadcasted_iota(I32, (rows, GROUPS * CAP), 0)
        pick = jnp.where(from_ref[...] == r, 1.0, 0.0).astype(BF16)
        out_ref[i * rows : (i + 1) * rows, :] = jnp.dot(pick, got_ref[...], preferred_element_type=F32).astype(BF16)


def body(queries, keys, values, gamma, w_merge, grids, positions):
    me = lax.axis_index(MLP)
    core = me % 2
    scal = jnp.stack([me, core, lax.axis_index("grp"), me]).astype(I32)
    shape = jax.ShapeDtypeStruct

    def move(x, perm):
        return lax.ppermute(x, MLP, perm)

    parts = []
    order = scal
    for chunk in range(CHUNKS):
        own, oth = rope(order, grids, queries, keys, values, chunk)
        if chunk == 1:
            w_merge, own, oth = lax.optimization_barrier((w_merge, own, oth))
            cols = lax.all_gather(w_merge, "zq", axis=0)
            own, oth, cols = lax.optimization_barrier((own, oth, cols))
            cols = lax.all_gather(cols, "grp", axis=0)
        order, own, oth = lax.optimization_barrier((order, own, oth))
        parts.append([own, move(oth, PART), move(own, SAME), move(oth, OPP)])

    tables = pl.pallas_call(
        layout_kernel,
        out_shape=[shape((NB * BLK, HD), BF16)] * 2 + [shape((2 * ROWS, NB * BLK), BF16)],
        in_specs=[smem(), smem()],
        out_specs=[vmem()] * 3,
        compiler_params=params(16),
        name="layout",
    )(scal, grids)
    to, frm = pl.pallas_call(
        index_kernel,
        out_shape=[shape((1, GPOOL), I32), shape((1, GROUPS * CAP), I32)],
        in_specs=[smem(), vmem()],
        out_specs=[vmem(), vmem()],
        compiler_params=params(24),
        name="index",
    )(scal, positions.reshape(GROUPS, GPOOL))
    owns, tables = lax.optimization_barrier(([p[0] for p in parts], tables))
    gains, _ = lax.optimization_barrier((jnp.broadcast_to(gamma[None, :], (2 * CHIPS, HD)), owns))
    gains = lax.all_to_all(gains, MLP, split_axis=0, concat_axis=0, tiled=True)
    gains = lax.dynamic_slice_in_dim(gains, core * CHIPS, CHIPS, 0).reshape(1, HALF).astype(F32)
    pooled = []
    for chunk in range(CHUNKS):
        mid, edge = attend([owns[chunk]] + parts[chunk][1:], tables)
        edge = move(edge, RING)
        pooled.append((mid, edge))
        tables, _ = lax.optimization_barrier((tables, edge))
    rows = jnp.concatenate([mid + edge for mid, edge in pooled], axis=1)
    rows = (rows.astype(F32) * gains).astype(BF16)
    below = move(rows, UP)
    above = move(rows, DOWN)
    last = move(below, UP)
    own = (below, rows, above, last)
    oth = [move(x, PART) for x in own]
    cols, to, frm, _ = lax.optimization_barrier((cols, to, frm, (below, above)))
    out = project(scal, own, oth, cols)
    out = lax.all_to_all(out, "zq", split_axis=0, concat_axis=0, tiled=True)

    out = pl.pallas_call(
        pack_kernel,
        out_shape=shape((GROUPS * CAP, HD), BF16),
        in_specs=[smem(), vmem(), vmem()],
        out_specs=vmem(),
        scratch_shapes=[pltpu.VMEM((GPOOL, HD), BF16)],
        compiler_params=params(24),
        name="pack",
    )(scal, to, out)
    out = lax.all_to_all(out, "grp", split_axis=0, concat_axis=0, tiled=True)
    return pl.pallas_call(
        place_kernel,
        out_shape=shape((GPOOL, HD), BF16),
        in_specs=[vmem(), vmem()],
        out_specs=vmem(),
        compiler_params=params(24),
        name="place",
    )(frm, out)


def solution(mesh):
    mesh = Mesh(mesh.devices.reshape(GROUPS, CHIPS // QUADS, QUADS, 2), ("grp",) + MLP)
    every = P(("grp",) + MLP, None)
    return jax.shard_map(
        body,
        mesh=mesh,
        in_specs=(every, every, every, P(MLP), P("grp", MLP), P("grp", None), P()),
        out_specs=P("grp", MLP),
        check_vma=False,
    )
```

```python
import math

import jax
import jax.numpy as jnp
from jax import lax
from jax.experimental import pallas as pl
from jax.experimental.pallas import tpu as pltpu
from jax.sharding import Mesh
from jax.sharding import PartitionSpec as P

HD = 128
HALF = 2048
IMGS = 16
BLK = 128
CHIPS = 16
CHUNKS = 2
HEADS = 8
WIDE = HEADS * HD
STEP = 4
NB = 4
ROWS = 64
CAP = 128
GROUPS = 16
GPOOL = 1024
SCALE = HD ** -0.5 / math.log(2.0)
F32 = jnp.float32
BF16 = jnp.bfloat16
I32 = jnp.int32
MLP = ("zq", "zr", "core")
WINDOW = (-1, 0, 1, -2)
QUADS = 4


def at(z, c):
    return (z % CHIPS) * 2 + c


SAME = [(at(z, 0), at(z - 1, 0)) for z in range(CHIPS)] + [(at(z, 1), at(z + 1, 1)) for z in range(CHIPS)]
OPP = [(at(z, 1), at(z - 1, 0)) for z in range(CHIPS)] + [(at(z, 0), at(z + 1, 1)) for z in range(CHIPS)]
RING = [(at(z, 0), at(z + 1, 0)) for z in range(CHIPS)] + [(at(z, 1), at(z - 1, 1)) for z in range(CHIPS)]
UP = [(at(z, c), at(z + 1, c)) for z in range(CHIPS) for c in range(2)]
DOWN = [(at(z, c), at(z - 1, c)) for z in range(CHIPS) for c in range(2)]
PART = [(at(z, c), at(z, 1 - c)) for z in range(CHIPS) for c in range(2)]


def vmem():
    return pl.BlockSpec(memory_space=pltpu.VMEM)


def smem():
    return pl.BlockSpec(memory_space=pltpu.SMEM)


def params(mib):
    return pltpu.CompilerParams(vmem_limit_bytes=mib << 20)


def cost(us):
    return pl.CostEstimate(flops=int(us * 1.15e9), bytes_accessed=int(us * 3.5e6), transcendentals=0)


def images_of(tok, grid_ref):
    image = jnp.where(tok < 0, -1, 0)
    first = jnp.zeros_like(tok)
    width = jnp.full_like(tok, grid_ref[0, 1])
    end = jnp.full_like(tok, grid_ref[0, 0] * grid_ref[0, 1])
    upto = jnp.int32(0)
    for n in range(IMGS):
        upto = upto + grid_ref[n, 0] * grid_ref[n, 1]
        past = tok >= upto
        image = jnp.where(past, n + 1, image)
        first = jnp.where(past, upto, first)
        if n + 1 < IMGS:
            width = jnp.where(past, grid_ref[n + 1, 1], width)
            end = jnp.where(past, upto + grid_ref[n + 1, 0] * grid_ref[n + 1, 1], end)
        else:
            width = jnp.where(past, 2, width)
    return image, first, width, end


def divide(a, b):
    return jnp.floor((a.astype(F32) + 0.5) / b.astype(F32)).astype(I32)


def rope_kernel(scal_ref, grid_ref, q_ref, k_ref, v_ref, *refs):
    outs = refs[: 2 * CHUNKS]
    cos_ref, sin_ref = refs[2 * CHUNKS :]
    lane = lax.broadcasted_iota(I32, (BLK, HD), 1)
    low = (lane % 64) < 32
    step = pl.program_id(0)

    @pl.when(step == 0)
    def _():
        tok = scal_ref[0] * BLK + lax.broadcasted_iota(I32, (BLK, HD), 0)
        _, first, width, _ = images_of(tok, grid_ref)
        local = tok - first
        row = divide(local, width)
        col = local - row * width
        freq = jnp.exp((lane % 32).astype(F32) * (-math.log(100.0) / 32.0))
        ang = jnp.where(lane < 64, row, col).astype(F32) * freq
        cos_ref[...] = jnp.cos(ang)
        sin = jnp.sin(ang)
        sin_ref[...] = jnp.where(low, -sin, sin)

    def fill(out_ref):
        cos = cos_ref[...]
        sin = sin_ref[...]
        for h in range(HEADS):
            lanes = slice(h * HD, (h + 1) * HD)
            for i, ref in ((0, q_ref), (1, k_ref)):
                x = ref[:, lanes].astype(F32)
                swap = jnp.where(low, pltpu.roll(x, 96, 1), pltpu.roll(x, 32, 1))
                out_ref[i, :, lanes] = (x * cos + swap * sin).astype(BF16)
        out_ref[2] = v_ref[...]

    for i in range(2 * CHUNKS):

        @pl.when(step == i)
        def _(out_ref=outs[i]):
            fill(out_ref)


def rope(scal, grids, queries, keys, values):
    queries, keys, values = (pltpu.with_memory_space_constraint(x, pltpu.HBM) for x in (queries, keys, values))

    def src(i, scal_ref):
        half = jnp.where(i % 2 == 0, scal_ref[1], 1 - scal_ref[1])
        return (0, half * (HALF // WIDE) + i // 2)

    outs = pl.pallas_call(
        rope_kernel,
        out_shape=[jax.ShapeDtypeStruct((3, BLK, WIDE), BF16)] * (2 * CHUNKS),
        grid_spec=pltpu.PrefetchScalarGridSpec(
            num_scalar_prefetch=1,
            grid=(2 * CHUNKS,),
            in_specs=[smem()] + [pl.BlockSpec((BLK, WIDE), src)] * 3,
            out_specs=[pl.BlockSpec((3, BLK, WIDE), lambda i, _: (0, 0, 0))] * (2 * CHUNKS),
            scratch_shapes=[pltpu.VMEM((BLK, HD), F32)] * 2,
        ),
        compiler_params=params(24),
        cost_estimate=cost(6),
        name="rope",
    )(scal, grids, queries, keys, values)
    return [outs[2 * c : 2 * c + 2] for c in range(CHUNKS)]


def layout_kernel(scal_ref, grid_ref, qhot_ref, khot_ref, pool_ref):
    chip = scal_ref[0] // 2
    core = scal_ref[1]
    lo = chip * 2 * BLK
    hi = lo + 2 * BLK
    for i in range(NB):
        tok = lo + BLK * jnp.where(core == 0, i, 1 - i) + lax.broadcasted_iota(I32, (BLK, HD), 0)
        image, _, _, _ = images_of(tok, grid_ref)
        hot = image + 1 == lax.broadcasted_iota(I32, (BLK, HD), 1)
        qhot_ref[i * BLK : (i + 1) * BLK, :] = jnp.where(hot, 256.0, 0.0).astype(BF16)
        khot_ref[i * BLK : (i + 1) * BLK, :] = jnp.where(hot, 128.0, 0.0).astype(BF16)
    lane = lax.broadcasted_iota(I32, (8, NB * BLK), 1)
    place = lane // BLK
    tok = lo + lane % BLK + BLK * jnp.where(core == 0, place, 1 - place)
    image, first, width, end = images_of(tok, grid_ref)
    local = tok - first
    prow = divide(jnp.maximum(local, 0), width)
    pcol = local - prow * width
    target = first // 4 + (prow // 2) * (width // 2) + pcol // 2
    begins = (first >= lo) & (first < hi)
    ends = (end > lo) & (end <= hi)
    owned = jnp.where(core == 0, begins.astype(I32), ends.astype(I32)) > 0
    target = jnp.where(owned & (image >= 0) & (image < IMGS), target, -1)[:1]
    r = lax.broadcasted_iota(I32, (2 * ROWS, NB * BLK), 0)
    far = jnp.where(core == 0, ROWS, -ROWS)
    mine = chip * ROWS + jnp.where(r < ROWS, r, r - ROWS + far)
    pool_ref[...] = jnp.where((target == mine) & (target >= 0), 1.0, 0.0).astype(BF16)


def attend_kernel(a_ref, b_ref, c_ref, d_ref, qhot_ref, khot_ref, pool_ref, mid_ref, edge_ref):
    refs = (a_ref, b_ref, c_ref, d_ref)
    pairs = NB // 2
    ones = jnp.ones((16, NB * BLK), BF16)
    nt = (((1,), (1,)), ((), ()))

    def score(h, i):
        lanes = slice(h * HD, (h + 1) * HD)
        keys = jnp.concatenate([ref[1, :, lanes] for ref in refs], axis=0)
        keys = jnp.concatenate([keys, khot_ref[...]], axis=1)
        q = jnp.concatenate([ref[0, :, lanes] for ref in refs[2 * i : 2 * i + 2]], axis=0)
        q = jnp.concatenate([q, qhot_ref[i * 2 * BLK : (i + 1) * 2 * BLK, :]], axis=1)
        return lax.dot_general(keys, q, nt, preferred_element_type=F32)

    def mix(h, s):
        lanes = slice(h * HD, (h + 1) * HD)
        e = jnp.exp2((s - jnp.max(s, axis=0, keepdims=True)) * SCALE).astype(BF16)
        vals = jnp.concatenate([ref[2, :, lanes] for ref in refs], axis=0)
        o = jnp.dot(jnp.concatenate([vals.T, ones], axis=0), e, preferred_element_type=F32)
        return (o[:HD] / o[HD : HD + 1]).astype(BF16)

    order = [(h, i) for h in range(STEP) for i in range(pairs)]
    later = score(*order[0])
    done = []
    for t, (h, i) in enumerate(order):
        now = later
        if t + 1 < len(order):
            later = score(*order[t + 1])
        done.append(mix(h, now))
        if len(done) == pairs:
            branch = jnp.concatenate(done, axis=1)
            done = []
            pooled = lax.dot_general(pool_ref[...], branch, nt, preferred_element_type=F32)
            pooled = (0.25 * pooled).astype(BF16)
            lanes = slice(h * HD, (h + 1) * HD)
            mid_ref[:, lanes] = pooled[:ROWS]
            edge_ref[:, lanes] = pooled[ROWS:]


def attend(parts, tables):
    part = pl.BlockSpec((3, BLK, STEP * HD), lambda h: (0, 0, h))
    tables = [pltpu.with_memory_space_constraint(t, pltpu.HBM) for t in tables]
    whole = [pl.BlockSpec(t.shape, lambda h: (0, 0)) for t in tables]
    return pl.pallas_call(
        attend_kernel,
        grid=(HEADS // STEP,),
        out_shape=[jax.ShapeDtypeStruct((ROWS, WIDE), BF16)] * 2,
        in_specs=[part] * NB + whole,
        out_specs=[pl.BlockSpec((ROWS, STEP * HD), lambda h: (0, h))] * 2,
        compiler_params=params(32),
        cost_estimate=cost(6),
        name="attend",
    )(*parts, *tables)


def project_kernel(scal_ref, *refs):
    w_own_ref, w_oth_ref, out_ref = refs[-3:]
    own = jnp.concatenate([ref[...] for ref in refs[:NB]], axis=0)
    oth = jnp.concatenate([ref[...] for ref in refs[NB : 2 * NB]], axis=0)

    def pair(ref):
        return jnp.concatenate([ref[:, i].reshape(HALF, HD) for i in range(2)], axis=1)

    total = jnp.dot(own, pair(w_own_ref), preferred_element_type=F32)
    total += jnp.dot(oth, pair(w_oth_ref), preferred_element_type=F32)
    for i in range(2):
        out_ref[i] = total[:, i * HD : (i + 1) * HD].astype(BF16)


def project(scal, own, oth, cols):
    rows = NB * ROWS
    half = (GROUPS // 2, 2, 2 * BLK, HD)
    cols = pltpu.with_memory_space_constraint(cols, pltpu.HBM)
    return pl.pallas_call(
        project_kernel,
        out_shape=jax.ShapeDtypeStruct((QUADS, rows, HD), BF16),
        grid_spec=pltpu.PrefetchScalarGridSpec(
            num_scalar_prefetch=1,
            grid=(QUADS // 2,),
            in_specs=[pl.BlockSpec((ROWS, HALF), lambda j, _: (0, 0))] * (2 * NB)
            + [
                pl.BlockSpec(half, lambda j, s: (s[1], j, 0, 0)),
                pl.BlockSpec(half, lambda j, s: (1 - s[1], j, 0, 0)),
            ],
            out_specs=pl.BlockSpec((2, rows, HD), lambda j, _: (j, 0, 0)),
        ),
        compiler_params=params(24),
        cost_estimate=cost(4),
        name="project",
    )(scal, *own, *oth, cols, cols)


def index_kernel(scal_ref, pos_ref, to_ref, from_ref):
    group = scal_ref[2]
    i = lax.broadcasted_iota(I32, (GPOOL, GPOOL), 0)
    j = lax.broadcasted_iota(I32, (GPOOL, GPOOL), 1)
    before = jnp.where(i < j, 1.0, 0.0).astype(BF16)
    own = pos_ref[pl.ds(group, 1), :] // GPOOL
    hot = (own == lax.broadcasted_iota(I32, (GROUPS, GPOOL), 0)).astype(F32)
    count = jnp.dot(hot.astype(BF16), before, preferred_element_type=F32)
    rank = jnp.sum(hot * count, axis=0, keepdims=True)
    to_ref[...] = own * CAP + rank.astype(I32)
    pos = pos_ref[...]
    here = pos // GPOOL == group
    rank = jnp.dot(here.astype(F32).astype(BF16), before, preferred_element_type=F32).astype(I32)
    rank = jnp.where(here, rank, -1)
    local = pos % GPOOL + 1
    high = (local // 32).astype(F32)
    low = (local % 32).astype(F32)
    r = lax.broadcasted_iota(I32, (CAP, GPOOL), 0)
    for g in range(GROUPS):
        pick = (rank[g : g + 1] == r).astype(F32).astype(BF16)
        pair = jnp.concatenate([high[g : g + 1], low[g : g + 1], jnp.zeros((6, GPOOL), F32)], axis=0)
        got = lax.dot_general(pair.astype(BF16), pick, (((1,), (1,)), ((), ())), preferred_element_type=F32)
        value = got[0:1] * 32.0 + got[1:2] - 1.0
        from_ref[:, g * CAP : (g + 1) * CAP] = value.astype(I32)


def pack_kernel(scal_ref, to_ref, got_ref, out_ref, all_ref):
    chip = scal_ref[0] // 2
    for k in range(QUADS):
        source = chip % QUADS + QUADS * k
        for i, off in enumerate(WINDOW):
            row = ((source + off + CHIPS) % CHIPS) * ROWS
            all_ref[pl.ds(pl.multiple_of(row, ROWS), ROWS), :] = got_ref[k, i * ROWS : (i + 1) * ROWS, :]
    rows = 256
    for i in range(GROUPS * CAP // rows):
        r = i * rows + lax.broadcasted_iota(I32, (rows, GPOOL), 0)
        pick = jnp.where(to_ref[...] == r, 1.0, 0.0).astype(BF16)
        out_ref[i * rows : (i + 1) * rows, :] = jnp.dot(pick, all_ref[...], preferred_element_type=F32).astype(BF16)


def place_kernel(from_ref, got_ref, out_ref):
    rows = 256
    for i in range(GPOOL // rows):
        r = i * rows + lax.broadcasted_iota(I32, (rows, GROUPS * CAP), 0)
        pick = jnp.where(from_ref[...] == r, 1.0, 0.0).astype(BF16)
        out_ref[i * rows : (i + 1) * rows, :] = jnp.dot(pick, got_ref[...], preferred_element_type=F32).astype(BF16)


def body(queries, keys, values, gamma, w_merge, grids, positions):
    me = lax.axis_index(MLP)
    core = me % 2
    scal = jnp.stack([me, core, lax.axis_index("grp"), me]).astype(I32)
    shape = jax.ShapeDtypeStruct

    def move(x, perm):
        return lax.ppermute(x, MLP, perm)

    halves = rope(scal, grids, queries, keys, values)
    w_merge, halves = lax.optimization_barrier((w_merge, halves))
    cols = lax.all_gather(w_merge, "zq", axis=0)
    halves, cols = lax.optimization_barrier((halves, cols))
    cols = lax.all_gather(cols, "grp", axis=0)
    parts = [[own, move(oth, PART), move(own, SAME), move(oth, OPP)] for own, oth in halves]

    tables = pl.pallas_call(
        layout_kernel,
        out_shape=[shape((NB * BLK, HD), BF16)] * 2 + [shape((2 * ROWS, NB * BLK), BF16)],
        in_specs=[smem(), smem()],
        out_specs=[vmem()] * 3,
        compiler_params=params(16),
        name="layout",
    )(scal, grids)
    to, frm = pl.pallas_call(
        index_kernel,
        out_shape=[shape((1, GPOOL), I32), shape((1, GROUPS * CAP), I32)],
        in_specs=[smem(), vmem()],
        out_specs=[vmem(), vmem()],
        compiler_params=params(24),
        name="index",
    )(scal, positions.reshape(GROUPS, GPOOL))
    gains, _ = lax.optimization_barrier((jnp.broadcast_to(gamma[None, :], (2 * CHIPS, HD)), halves))
    gains = lax.all_to_all(gains, MLP, split_axis=0, concat_axis=0, tiled=True)
    gains = lax.dynamic_slice_in_dim(gains, core * CHIPS, CHIPS, 0).reshape(1, HALF).astype(F32)
    owns, tables, to, frm, gains = lax.optimization_barrier(([p[0] for p in parts], tables, to, frm, gains))
    pooled = []
    for chunk in range(CHUNKS):
        mid, edge = attend([owns[chunk]] + parts[chunk][1:], tables)
        edge = move(edge, RING)
        pooled.append((mid, edge))
        tables, _ = lax.optimization_barrier((tables, edge))
    rows = jnp.concatenate([mid + edge for mid, edge in pooled], axis=1)
    rows = (rows.astype(F32) * gains).astype(BF16)
    below = move(rows, UP)
    above = move(rows, DOWN)
    last = move(below, UP)
    own = (below, rows, above, last)
    oth = [move(x, PART) for x in own]
    cols, _ = lax.optimization_barrier((cols, (below, above)))
    out = project(scal, own, oth, cols)
    out = lax.all_to_all(out, "zq", split_axis=0, concat_axis=0, tiled=True)

    out = pl.pallas_call(
        pack_kernel,
        out_shape=shape((GROUPS * CAP, HD), BF16),
        in_specs=[smem(), vmem(), vmem()],
        out_specs=vmem(),
        scratch_shapes=[pltpu.VMEM((GPOOL, HD), BF16)],
        compiler_params=params(24),
        name="pack",
    )(scal, to, out)
    out = lax.all_to_all(out, "grp", split_axis=0, concat_axis=0, tiled=True)
    return pl.pallas_call(
        place_kernel,
        out_shape=shape((GPOOL, HD), BF16),
        in_specs=[vmem(), vmem()],
        out_specs=vmem(),
        compiler_params=params(24),
        name="place",
    )(frm, out)


def solution(mesh):
    mesh = Mesh(mesh.devices.reshape(GROUPS, CHIPS // QUADS, QUADS, 2), ("grp",) + MLP)
    every = P(("grp",) + MLP, None)
    return jax.shard_map(
        body,
        mesh=mesh,
        in_specs=(every, every, every, P(MLP), P("grp", MLP), P("grp", None), P()),
        out_specs=P("grp", MLP),
        check_vma=False,
    )
```

```python
import math

import jax
import jax.numpy as jnp
from jax import lax
from jax.experimental import pallas as pl
from jax.experimental.pallas import tpu as pltpu
from jax.sharding import Mesh
from jax.sharding import PartitionSpec as P

HD = 128
HALF = 2048
IMGS = 16
BLK = 128
CHIPS = 16
CHUNKS = 2
HEADS = 8
WIDE = HEADS * HD
STEP = 4
NB = 4
ROWS = 64
CAP = 128
GROUPS = 16
GPOOL = 1024
SCALE = HD ** -0.5 / math.log(2.0)
F32 = jnp.float32
BF16 = jnp.bfloat16
I32 = jnp.int32
MLP = ("zq", "zr", "core")
WINDOW = (-1, 0, 1, -2)
QUADS = 4


def at(z, c):
    return (z % CHIPS) * 2 + c


SAME = [(at(z, 0), at(z - 1, 0)) for z in range(CHIPS)] + [(at(z, 1), at(z + 1, 1)) for z in range(CHIPS)]
OPP = [(at(z, 1), at(z - 1, 0)) for z in range(CHIPS)] + [(at(z, 0), at(z + 1, 1)) for z in range(CHIPS)]
RING = [(at(z, 0), at(z + 1, 0)) for z in range(CHIPS)] + [(at(z, 1), at(z - 1, 1)) for z in range(CHIPS)]
UP = [(at(z, c), at(z + 1, c)) for z in range(CHIPS) for c in range(2)]
DOWN = [(at(z, c), at(z - 1, c)) for z in range(CHIPS) for c in range(2)]
PART = [(at(z, c), at(z, 1 - c)) for z in range(CHIPS) for c in range(2)]


def vmem():
    return pl.BlockSpec(memory_space=pltpu.VMEM)


def smem():
    return pl.BlockSpec(memory_space=pltpu.SMEM)


def params(mib):
    return pltpu.CompilerParams(vmem_limit_bytes=mib << 20)


def cost(us):
    return pl.CostEstimate(flops=int(us * 1.15e9), bytes_accessed=int(us * 3.5e6), transcendentals=0)


def images_of(tok, grid_ref):
    image = jnp.where(tok < 0, -1, 0)
    first = jnp.zeros_like(tok)
    width = jnp.full_like(tok, grid_ref[0, 1])
    end = jnp.full_like(tok, grid_ref[0, 0] * grid_ref[0, 1])
    upto = jnp.int32(0)
    for n in range(IMGS):
        upto = upto + grid_ref[n, 0] * grid_ref[n, 1]
        past = tok >= upto
        image = jnp.where(past, n + 1, image)
        first = jnp.where(past, upto, first)
        if n + 1 < IMGS:
            width = jnp.where(past, grid_ref[n + 1, 1], width)
            end = jnp.where(past, upto + grid_ref[n + 1, 0] * grid_ref[n + 1, 1], end)
        else:
            width = jnp.where(past, 2, width)
    return image, first, width, end


def divide(a, b):
    return jnp.floor((a.astype(F32) + 0.5) / b.astype(F32)).astype(I32)


def rope_kernel(scal_ref, grid_ref, q_ref, k_ref, v_ref, *refs):
    outs = refs[: 2 * CHUNKS]
    cos_ref, sin_ref = refs[2 * CHUNKS :]
    lane = lax.broadcasted_iota(I32, (BLK, HD), 1)
    low = (lane % 64) < 32
    step = pl.program_id(0)

    @pl.when(step == 0)
    def _():
        tok = scal_ref[0] * BLK + lax.broadcasted_iota(I32, (BLK, HD), 0)
        _, first, width, _ = images_of(tok, grid_ref)
        local = tok - first
        row = divide(local, width)
        col = local - row * width
        freq = jnp.exp((lane % 32).astype(F32) * (-math.log(100.0) / 32.0))
        ang = jnp.where(lane < 64, row, col).astype(F32) * freq
        cos_ref[...] = jnp.cos(ang)
        sin = jnp.sin(ang)
        sin_ref[...] = jnp.where(low, -sin, sin)

    def fill(out_ref):
        cos = cos_ref[...]
        sin = sin_ref[...]
        for h in range(HEADS):
            lanes = slice(h * HD, (h + 1) * HD)
            for i, ref in ((0, q_ref), (1, k_ref)):
                x = ref[:, lanes].astype(F32)
                swap = jnp.where(low, pltpu.roll(x, 96, 1), pltpu.roll(x, 32, 1))
                out_ref[i, :, lanes] = (x * cos + swap * sin).astype(BF16)
        out_ref[2] = v_ref[...]

    for i in range(2 * CHUNKS):

        @pl.when(step == i)
        def _(out_ref=outs[i]):
            fill(out_ref)


def rope(scal, grids, queries, keys, values):
    queries, keys, values = (pltpu.with_memory_space_constraint(x, pltpu.HBM) for x in (queries, keys, values))

    def src(i, scal_ref):
        half = jnp.where(i % 2 == 0, scal_ref[1], 1 - scal_ref[1])
        return (0, half * (HALF // WIDE) + i // 2)

    outs = pl.pallas_call(
        rope_kernel,
        out_shape=[jax.ShapeDtypeStruct((3, BLK, WIDE), BF16)] * (2 * CHUNKS),
        grid_spec=pltpu.PrefetchScalarGridSpec(
            num_scalar_prefetch=1,
            grid=(2 * CHUNKS,),
            in_specs=[smem()] + [pl.BlockSpec((BLK, WIDE), src)] * 3,
            out_specs=[pl.BlockSpec((3, BLK, WIDE), lambda i, _: (0, 0, 0))] * (2 * CHUNKS),
            scratch_shapes=[pltpu.VMEM((BLK, HD), F32)] * 2,
        ),
        compiler_params=params(24),
        cost_estimate=cost(6),
        name="rope",
    )(scal, grids, queries, keys, values)
    return [outs[2 * c : 2 * c + 2] for c in range(CHUNKS)]


def layout_kernel(scal_ref, grid_ref, qhot_ref, khot_ref, pool_ref):
    chip = scal_ref[0] // 2
    core = scal_ref[1]
    lo = chip * 2 * BLK
    hi = lo + 2 * BLK
    for i in range(NB):
        tok = lo + BLK * jnp.where(core == 0, i, 1 - i) + lax.broadcasted_iota(I32, (BLK, HD), 0)
        image, _, _, _ = images_of(tok, grid_ref)
        hot = image + 1 == lax.broadcasted_iota(I32, (BLK, HD), 1)
        qhot_ref[i * BLK : (i + 1) * BLK, :] = jnp.where(hot, 256.0, 0.0).astype(BF16)
        khot_ref[i * BLK : (i + 1) * BLK, :] = jnp.where(hot, 128.0, 0.0).astype(BF16)
    lane = lax.broadcasted_iota(I32, (8, NB * BLK), 1)
    place = lane // BLK
    tok = lo + lane % BLK + BLK * jnp.where(core == 0, place, 1 - place)
    image, first, width, end = images_of(tok, grid_ref)
    local = tok - first
    prow = divide(jnp.maximum(local, 0), width)
    pcol = local - prow * width
    target = first // 4 + (prow // 2) * (width // 2) + pcol // 2
    begins = (first >= lo) & (first < hi)
    ends = (end > lo) & (end <= hi)
    owned = jnp.where(core == 0, begins.astype(I32), ends.astype(I32)) > 0
    target = jnp.where(owned & (image >= 0) & (image < IMGS), target, -1)[:1]
    r = lax.broadcasted_iota(I32, (2 * ROWS, NB * BLK), 0)
    far = jnp.where(core == 0, ROWS, -ROWS)
    mine = chip * ROWS + jnp.where(r < ROWS, r, r - ROWS + far)
    pool_ref[...] = jnp.where((target == mine) & (target >= 0), 1.0, 0.0).astype(BF16)


def attend_kernel(a_ref, b_ref, c_ref, d_ref, qhot_ref, khot_ref, pool_ref, mid_ref, edge_ref):
    refs = (a_ref, b_ref, c_ref, d_ref)
    pairs = NB // 2
    ones = jnp.ones((16, NB * BLK), BF16)
    nt = (((1,), (1,)), ((), ()))

    def score(h, i):
        lanes = slice(h * HD, (h + 1) * HD)
        keys = jnp.concatenate([ref[1, :, lanes] for ref in refs], axis=0)
        keys = jnp.concatenate([keys, khot_ref[...]], axis=1)
        q = jnp.concatenate([ref[0, :, lanes] for ref in refs[2 * i : 2 * i + 2]], axis=0)
        q = jnp.concatenate([q, qhot_ref[i * 2 * BLK : (i + 1) * 2 * BLK, :]], axis=1)
        return lax.dot_general(keys, q, nt, preferred_element_type=F32)

    def mix(h, s):
        lanes = slice(h * HD, (h + 1) * HD)
        e = jnp.exp2((s - jnp.max(s, axis=0, keepdims=True)) * SCALE).astype(BF16)
        vals = jnp.concatenate([ref[2, :, lanes] for ref in refs], axis=0)
        o = jnp.dot(jnp.concatenate([vals.T, ones], axis=0), e, preferred_element_type=F32)
        return (o[:HD] / o[HD : HD + 1]).astype(BF16)

    order = [(h, i) for h in range(STEP) for i in range(pairs)]
    later = score(*order[0])
    done = []
    for t, (h, i) in enumerate(order):
        now = later
        if t + 1 < len(order):
            later = score(*order[t + 1])
        done.append(mix(h, now))
        if len(done) == pairs:
            branch = jnp.concatenate(done, axis=1)
            done = []
            pooled = lax.dot_general(pool_ref[...], branch, nt, preferred_element_type=F32)
            pooled = (0.25 * pooled).astype(BF16)
            lanes = slice(h * HD, (h + 1) * HD)
            mid_ref[:, lanes] = pooled[:ROWS]
            edge_ref[:, lanes] = pooled[ROWS:]


def attend(parts, tables):
    part = pl.BlockSpec((3, BLK, STEP * HD), lambda h: (0, 0, h))
    tables = [pltpu.with_memory_space_constraint(t, pltpu.HBM) for t in tables]
    whole = [pl.BlockSpec(t.shape, lambda h: (0, 0)) for t in tables]
    return pl.pallas_call(
        attend_kernel,
        grid=(HEADS // STEP,),
        out_shape=[jax.ShapeDtypeStruct((ROWS, WIDE), BF16)] * 2,
        in_specs=[part] * NB + whole,
        out_specs=[pl.BlockSpec((ROWS, STEP * HD), lambda h: (0, h))] * 2,
        compiler_params=params(32),
        cost_estimate=cost(6),
        name="attend",
    )(*parts, *tables)


def project_kernel(scal_ref, *refs):
    w_own_ref, w_oth_ref, out_ref = refs[-3:]
    own = jnp.concatenate([ref[...] for ref in refs[:NB]], axis=0)
    oth = jnp.concatenate([ref[...] for ref in refs[NB : 2 * NB]], axis=0)

    def pair(ref):
        return jnp.concatenate([ref[:, i].reshape(HALF, HD) for i in range(2)], axis=1)

    total = jnp.dot(own, pair(w_own_ref), preferred_element_type=F32)
    total += jnp.dot(oth, pair(w_oth_ref), preferred_element_type=F32)
    for i in range(2):
        out_ref[i] = total[:, i * HD : (i + 1) * HD].astype(BF16)


def project(scal, own, oth, cols):
    rows = NB * ROWS
    half = (GROUPS // 2, 2, 2 * BLK, HD)
    cols = pltpu.with_memory_space_constraint(cols, pltpu.HBM)
    return pl.pallas_call(
        project_kernel,
        out_shape=jax.ShapeDtypeStruct((QUADS, rows, HD), BF16),
        grid_spec=pltpu.PrefetchScalarGridSpec(
            num_scalar_prefetch=1,
            grid=(QUADS // 2,),
            in_specs=[pl.BlockSpec((ROWS, HALF), lambda j, _: (0, 0))] * (2 * NB)
            + [
                pl.BlockSpec(half, lambda j, s: (s[1], j, 0, 0)),
                pl.BlockSpec(half, lambda j, s: (1 - s[1], j, 0, 0)),
            ],
            out_specs=pl.BlockSpec((2, rows, HD), lambda j, _: (j, 0, 0)),
        ),
        compiler_params=params(24),
        cost_estimate=cost(4),
        name="project",
    )(scal, *own, *oth, cols, cols)


def index_kernel(scal_ref, pos_ref, to_ref, from_ref):
    group = scal_ref[2]
    i = lax.broadcasted_iota(I32, (GPOOL, GPOOL), 0)
    j = lax.broadcasted_iota(I32, (GPOOL, GPOOL), 1)
    before = jnp.where(i < j, 1.0, 0.0).astype(BF16)
    own = pos_ref[pl.ds(group, 1), :] // GPOOL
    hot = (own == lax.broadcasted_iota(I32, (GROUPS, GPOOL), 0)).astype(F32)
    count = jnp.dot(hot.astype(BF16), before, preferred_element_type=F32)
    rank = jnp.sum(hot * count, axis=0, keepdims=True)
    to_ref[...] = own * CAP + rank.astype(I32)
    pos = pos_ref[...]
    here = pos // GPOOL == group
    rank = jnp.dot(here.astype(F32).astype(BF16), before, preferred_element_type=F32).astype(I32)
    rank = jnp.where(here, rank, -1)
    local = pos % GPOOL + 1
    high = (local // 32).astype(F32)
    low = (local % 32).astype(F32)
    r = lax.broadcasted_iota(I32, (CAP, GPOOL), 0)
    for g in range(GROUPS):
        pick = (rank[g : g + 1] == r).astype(F32).astype(BF16)
        pair = jnp.concatenate([high[g : g + 1], low[g : g + 1], jnp.zeros((6, GPOOL), F32)], axis=0)
        got = lax.dot_general(pair.astype(BF16), pick, (((1,), (1,)), ((), ())), preferred_element_type=F32)
        value = got[0:1] * 32.0 + got[1:2] - 1.0
        from_ref[:, g * CAP : (g + 1) * CAP] = value.astype(I32)


def pack_kernel(scal_ref, to_ref, got_ref, out_ref, all_ref):
    chip = scal_ref[0] // 2
    for k in range(QUADS):
        source = chip % QUADS + QUADS * k
        for i, off in enumerate(WINDOW):
            row = ((source + off + CHIPS) % CHIPS) * ROWS
            all_ref[pl.ds(pl.multiple_of(row, ROWS), ROWS), :] = got_ref[k, i * ROWS : (i + 1) * ROWS, :]
    rows = 256
    for i in range(GROUPS * CAP // rows):
        r = i * rows + lax.broadcasted_iota(I32, (rows, GPOOL), 0)
        pick = jnp.where(to_ref[...] == r, 1.0, 0.0).astype(BF16)
        out_ref[i * rows : (i + 1) * rows, :] = jnp.dot(pick, all_ref[...], preferred_element_type=F32).astype(BF16)


def place_kernel(from_ref, got_ref, out_ref):
    rows = 256
    for i in range(GPOOL // rows):
        r = i * rows + lax.broadcasted_iota(I32, (rows, GROUPS * CAP), 0)
        pick = jnp.where(from_ref[...] == r, 1.0, 0.0).astype(BF16)
        out_ref[i * rows : (i + 1) * rows, :] = jnp.dot(pick, got_ref[...], preferred_element_type=F32).astype(BF16)


def body(queries, keys, values, gamma, w_merge, grids, positions):
    me = lax.axis_index(MLP)
    core = me % 2
    scal = jnp.stack([me, core, lax.axis_index("grp"), me]).astype(I32)
    shape = jax.ShapeDtypeStruct

    def move(x, perm):
        return lax.ppermute(x, MLP, perm)

    halves = rope(scal, grids, queries, keys, values)
    w_merge, halves = lax.optimization_barrier((w_merge, halves))
    cols = lax.all_gather(w_merge, "zq", axis=0)
    halves, cols = lax.optimization_barrier((halves, cols))
    cols = lax.all_gather(cols, "grp", axis=0)
    parts = [[own, move(oth, PART), move(own, SAME), move(oth, OPP)] for own, oth in halves]

    tables = pl.pallas_call(
        layout_kernel,
        out_shape=[pltpu.HBM((NB * BLK, HD), BF16)] * 2 + [pltpu.HBM((2 * ROWS, NB * BLK), BF16)],
        in_specs=[smem(), smem()],
        out_specs=[vmem()] * 3,
        compiler_params=params(16),
        name="layout",
    )(scal, grids)
    gains, parts[-1][1] = lax.optimization_barrier((jnp.broadcast_to(gamma[None, :], (2 * CHIPS, HD)), parts[-1][1]))
    gains = lax.all_to_all(gains, MLP, split_axis=0, concat_axis=0, tiled=True)
    gains = lax.dynamic_slice_in_dim(gains, core * CHIPS, CHIPS, 0).reshape(1, HALF).astype(F32)
    owns, tables, gains = lax.optimization_barrier(([p[0] for p in parts], tables, gains))
    pooled = []
    for chunk in range(CHUNKS):
        mid, edge = attend([owns[chunk]] + parts[chunk][1:], tables)
        edge = move(edge, RING)
        pooled.append((mid, edge))
        if chunk == 0:
            positions, _ = lax.optimization_barrier((positions, mid))
            to, frm = pl.pallas_call(
                index_kernel,
                out_shape=[shape((1, GPOOL), I32), shape((1, GROUPS * CAP), I32)],
                in_specs=[smem(), vmem()],
                out_specs=[vmem(), vmem()],
                compiler_params=params(24),
                name="index",
            )(scal, positions.reshape(GROUPS, GPOOL))
            tables, to, frm, _ = lax.optimization_barrier((tables, to, frm, edge))
    rows = jnp.concatenate([mid + edge for mid, edge in pooled], axis=1)
    rows = (rows.astype(F32) * gains).astype(BF16)
    below = move(rows, UP)
    above = move(rows, DOWN)
    last = move(below, UP)
    own = (below, rows, above, last)
    oth = [move(x, PART) for x in own]
    cols, _ = lax.optimization_barrier((cols, (below, above)))
    out = project(scal, own, oth, cols)
    out = lax.all_to_all(out, "zq", split_axis=0, concat_axis=0, tiled=True)

    out = pl.pallas_call(
        pack_kernel,
        out_shape=shape((GROUPS * CAP, HD), BF16),
        in_specs=[smem(), vmem(), vmem()],
        out_specs=vmem(),
        scratch_shapes=[pltpu.VMEM((GPOOL, HD), BF16)],
        compiler_params=params(24),
        name="pack",
    )(scal, to, out)
    out = lax.all_to_all(out, "grp", split_axis=0, concat_axis=0, tiled=True)
    return pl.pallas_call(
        place_kernel,
        out_shape=shape((GPOOL, HD), BF16),
        in_specs=[vmem(), vmem()],
        out_specs=vmem(),
        compiler_params=params(24),
        name="place",
    )(frm, out)


def solution(mesh):
    mesh = Mesh(mesh.devices.reshape(GROUPS, CHIPS // QUADS, QUADS, 2), ("grp",) + MLP)
    every = P(("grp",) + MLP, None)
    return jax.shard_map(
        body,
        mesh=mesh,
        in_specs=(every, every, every, P(MLP), P("grp", MLP), P("grp", None), P()),
        out_specs=P("grp", MLP),
        check_vma=False,
    )
```

```python
import math

import jax
import jax.numpy as jnp
from jax import lax
from jax.experimental import pallas as pl
from jax.experimental.pallas import tpu as pltpu
from jax.sharding import Mesh
from jax.sharding import PartitionSpec as P

HD = 128
HALF = 2048
IMGS = 16
BLK = 128
CHIPS = 16
CHUNKS = 2
HEADS = 8
WIDE = HEADS * HD
STEP = 4
NB = 4
ROWS = 64
CAP = 128
GROUPS = 16
GPOOL = 1024
SCALE = HD ** -0.5 / math.log(2.0)
F32 = jnp.float32
BF16 = jnp.bfloat16
I32 = jnp.int32
MLP = ("zq", "zr", "core")
WINDOW = (-1, 0, 1, -2)
QUADS = 4


def at(z, c):
    return (z % CHIPS) * 2 + c


SAME = [(at(z, 0), at(z - 1, 0)) for z in range(CHIPS)] + [(at(z, 1), at(z + 1, 1)) for z in range(CHIPS)]
OPP = [(at(z, 1), at(z - 1, 0)) for z in range(CHIPS)] + [(at(z, 0), at(z + 1, 1)) for z in range(CHIPS)]
RING = [(at(z, 0), at(z + 1, 0)) for z in range(CHIPS)] + [(at(z, 1), at(z - 1, 1)) for z in range(CHIPS)]
UP = [(at(z, c), at(z + 1, c)) for z in range(CHIPS) for c in range(2)]
DOWN = [(at(z, c), at(z - 1, c)) for z in range(CHIPS) for c in range(2)]
PART = [(at(z, c), at(z, 1 - c)) for z in range(CHIPS) for c in range(2)]


def vmem():
    return pl.BlockSpec(memory_space=pltpu.VMEM)


def smem():
    return pl.BlockSpec(memory_space=pltpu.SMEM)


def params(mib):
    return pltpu.CompilerParams(vmem_limit_bytes=mib << 20)


def cost(us):
    return pl.CostEstimate(flops=int(us * 1.15e9), bytes_accessed=int(us * 3.5e6), transcendentals=0)


def images_of(tok, grid_ref):
    image = jnp.where(tok < 0, -1, 0)
    first = jnp.zeros_like(tok)
    width = jnp.full_like(tok, grid_ref[1, 0])
    end = jnp.full_like(tok, grid_ref[0, 0] * grid_ref[1, 0])
    upto = jnp.int32(0)
    for n in range(IMGS):
        upto = upto + grid_ref[0, n] * grid_ref[1, n]
        past = tok >= upto
        image = jnp.where(past, n + 1, image)
        first = jnp.where(past, upto, first)
        if n + 1 < IMGS:
            width = jnp.where(past, grid_ref[1, n + 1], width)
            end = jnp.where(past, upto + grid_ref[0, n + 1] * grid_ref[1, n + 1], end)
        else:
            width = jnp.where(past, 2, width)
    return image, first, width, end


def divide(a, b):
    return jnp.floor((a.astype(F32) + 0.5) / b.astype(F32)).astype(I32)


def rope_kernel(scal_ref, grid_ref, q_ref, k_ref, v_ref, *refs):
    outs = refs[: 2 * CHUNKS]
    cos_ref, sin_ref = refs[2 * CHUNKS :]
    lane = lax.broadcasted_iota(I32, (BLK, HD), 1)
    low = (lane % 64) < 32
    step = pl.program_id(0)

    @pl.when(step == 0)
    def _():
        tok = scal_ref[0] * BLK + lax.broadcasted_iota(I32, (BLK, HD), 0)
        _, first, width, _ = images_of(tok, grid_ref)
        local = tok - first
        row = divide(local, width)
        col = local - row * width
        freq = jnp.exp((lane % 32).astype(F32) * (-math.log(100.0) / 32.0))
        ang = jnp.where(lane < 64, row, col).astype(F32) * freq
        cos_ref[...] = jnp.cos(ang)
        sin = jnp.sin(ang)
        sin_ref[...] = jnp.where(low, -sin, sin)

    def fill(out_ref):
        cos = cos_ref[...]
        sin = sin_ref[...]
        for h in range(HEADS):
            lanes = slice(h * HD, (h + 1) * HD)
            for i, ref in ((0, q_ref), (1, k_ref)):
                x = ref[:, lanes].astype(F32)
                swap = jnp.where(low, pltpu.roll(x, 96, 1), pltpu.roll(x, 32, 1))
                out_ref[i, :, lanes] = (x * cos + swap * sin).astype(BF16)
        out_ref[2] = v_ref[...]

    for i in range(2 * CHUNKS):

        @pl.when(step == i)
        def _(out_ref=outs[i]):
            fill(out_ref)


def rope(scal, grids, queries, keys, values):
    queries, keys, values = (pltpu.with_memory_space_constraint(x, pltpu.HBM) for x in (queries, keys, values))

    def src(i, scal_ref):
        half = jnp.where(i % 2 == 0, scal_ref[1], 1 - scal_ref[1])
        return (0, half * (HALF // WIDE) + i // 2)

    outs = pl.pallas_call(
        rope_kernel,
        out_shape=[pltpu.HBM((3, BLK, WIDE), BF16)] * (2 * CHUNKS),
        grid_spec=pltpu.PrefetchScalarGridSpec(
            num_scalar_prefetch=1,
            grid=(2 * CHUNKS,),
            in_specs=[smem()] + [pl.BlockSpec((BLK, WIDE), src)] * 3,
            out_specs=[pl.BlockSpec((3, BLK, WIDE), lambda i, _: (0, 0, 0))] * (2 * CHUNKS),
            scratch_shapes=[pltpu.VMEM((BLK, HD), F32)] * 2,
        ),
        compiler_params=params(24),
        cost_estimate=cost(6),
        name="rope",
    )(scal, grids, queries, keys, values)
    return [outs[2 * c : 2 * c + 2] for c in range(CHUNKS)]


def layout_kernel(scal_ref, grid_ref, qhot_ref, khot_ref, pool_ref):
    chip = scal_ref[0] // 2
    core = scal_ref[1]
    lo = chip * 2 * BLK
    hi = lo + 2 * BLK
    for i in range(NB):
        tok = lo + BLK * jnp.where(core == 0, i, 1 - i) + lax.broadcasted_iota(I32, (BLK, HD), 0)
        image, _, _, _ = images_of(tok, grid_ref)
        hot = image + 1 == lax.broadcasted_iota(I32, (BLK, HD), 1)
        qhot_ref[i * BLK : (i + 1) * BLK, :] = jnp.where(hot, 256.0, 0.0).astype(BF16)
        khot_ref[i * BLK : (i + 1) * BLK, :] = jnp.where(hot, 128.0, 0.0).astype(BF16)
    lane = lax.broadcasted_iota(I32, (8, NB * BLK), 1)
    place = lane // BLK
    tok = lo + lane % BLK + BLK * jnp.where(core == 0, place, 1 - place)
    image, first, width, end = images_of(tok, grid_ref)
    local = tok - first
    prow = divide(jnp.maximum(local, 0), width)
    pcol = local - prow * width
    target = first // 4 + (prow // 2) * (width // 2) + pcol // 2
    begins = (first >= lo) & (first < hi)
    ends = (end > lo) & (end <= hi)
    owned = jnp.where(core == 0, begins.astype(I32), ends.astype(I32)) > 0
    target = jnp.where(owned & (image >= 0) & (image < IMGS), target, -1)[:1]
    r = lax.broadcasted_iota(I32, (2 * ROWS, NB * BLK), 0)
    far = jnp.where(core == 0, ROWS, -ROWS)
    mine = chip * ROWS + jnp.where(r < ROWS, r, r - ROWS + far)
    pool_ref[...] = jnp.where((target == mine) & (target >= 0), 1.0, 0.0).astype(BF16)


def attend_kernel(a_ref, c_ref, d_ref, b_ref, qhot_ref, khot_ref, pool_ref, mid_ref, edge_ref):
    refs = (a_ref, b_ref, c_ref, d_ref)
    pairs = NB // 2
    ones = jnp.ones((16, NB * BLK), BF16)
    nt = (((1,), (1,)), ((), ()))

    def score(h, i):
        lanes = slice(h * HD, (h + 1) * HD)
        keys = jnp.concatenate([ref[1, :, lanes] for ref in refs], axis=0)
        keys = jnp.concatenate([keys, khot_ref[...]], axis=1)
        q = jnp.concatenate([ref[0, :, lanes] for ref in refs[2 * i : 2 * i + 2]], axis=0)
        q = jnp.concatenate([q, qhot_ref[i * 2 * BLK : (i + 1) * 2 * BLK, :]], axis=1)
        return lax.dot_general(keys, q, nt, preferred_element_type=F32)

    def mix(h, s):
        lanes = slice(h * HD, (h + 1) * HD)
        e = jnp.exp2((s - jnp.max(s, axis=0, keepdims=True)) * SCALE).astype(BF16)
        vals = jnp.concatenate([ref[2, :, lanes] for ref in refs], axis=0)
        o = jnp.dot(jnp.concatenate([vals.T, ones], axis=0), e, preferred_element_type=F32)
        return (o[:HD] / o[HD : HD + 1]).astype(BF16)

    order = [(h, i) for h in range(STEP) for i in range(pairs)]
    later = score(*order[0])
    done = []
    for t, (h, i) in enumerate(order):
        now = later
        if t + 1 < len(order):
            later = score(*order[t + 1])
        done.append(mix(h, now))
        if len(done) == pairs:
            branch = jnp.concatenate(done, axis=1)
            done = []
            pooled = lax.dot_general(pool_ref[...], branch, nt, preferred_element_type=F32)
            pooled = (0.25 * pooled).astype(BF16)
            lanes = slice(h * HD, (h + 1) * HD)
            mid_ref[:, lanes] = pooled[:ROWS]
            edge_ref[:, lanes] = pooled[ROWS:]


def attend(parts, tables):
    part = pl.BlockSpec((3, BLK, STEP * HD), lambda h: (0, 0, h))
    own, tables = ([pltpu.with_memory_space_constraint(t, pltpu.HBM) for t in x] for x in (parts[:1], tables))
    whole = [pl.BlockSpec(t.shape, lambda h: (0, 0)) for t in tables]
    return pl.pallas_call(
        attend_kernel,
        grid=(HEADS // STEP,),
        out_shape=[jax.ShapeDtypeStruct((ROWS, WIDE), BF16)] * 2,
        in_specs=[part] * NB + whole,
        out_specs=[pl.BlockSpec((ROWS, STEP * HD), lambda h: (0, h))] * 2,
        compiler_params=params(32),
        cost_estimate=cost(6),
        name="attend",
    )(*own, *parts[1:], *tables)


def project_kernel(scal_ref, *refs):
    w_own_ref, w_oth_ref, out_ref = refs[-3:]
    own = jnp.concatenate([ref[...] for ref in refs[:NB]], axis=0)
    oth = jnp.concatenate([ref[...] for ref in refs[NB : 2 * NB]], axis=0)

    def pair(ref):
        return jnp.concatenate([ref[:, i].reshape(HALF, HD) for i in range(2)], axis=1)

    total = jnp.dot(own, pair(w_own_ref), preferred_element_type=F32)
    total += jnp.dot(oth, pair(w_oth_ref), preferred_element_type=F32)
    for i in range(2):
        out_ref[i] = total[:, i * HD : (i + 1) * HD].astype(BF16)


def project(scal, own, oth, cols):
    rows = NB * ROWS
    half = (GROUPS // 2, 2, 2 * BLK, HD)
    cols = pltpu.with_memory_space_constraint(cols, pltpu.HBM)
    return pl.pallas_call(
        project_kernel,
        out_shape=jax.ShapeDtypeStruct((QUADS, rows, HD), BF16),
        grid_spec=pltpu.PrefetchScalarGridSpec(
            num_scalar_prefetch=1,
            grid=(QUADS // 2,),
            in_specs=[pl.BlockSpec((ROWS, HALF), lambda j, _: (0, 0))] * (2 * NB)
            + [
                pl.BlockSpec(half, lambda j, s: (s[1], j, 0, 0)),
                pl.BlockSpec(half, lambda j, s: (1 - s[1], j, 0, 0)),
            ],
            out_specs=pl.BlockSpec((2, rows, HD), lambda j, _: (j, 0, 0)),
        ),
        compiler_params=params(24),
        cost_estimate=cost(4),
        name="project",
    )(scal, *own, *oth, cols, cols)


def index_kernel(scal_ref, pos_ref, to_ref, from_ref):
    group = scal_ref[2]
    i = lax.broadcasted_iota(I32, (GPOOL, GPOOL), 0)
    j = lax.broadcasted_iota(I32, (GPOOL, GPOOL), 1)
    before = jnp.where(i < j, 1.0, 0.0).astype(BF16)
    own = pos_ref[pl.ds(group, 1), :] // GPOOL
    hot = (own == lax.broadcasted_iota(I32, (GROUPS, GPOOL), 0)).astype(F32)
    count = jnp.dot(hot.astype(BF16), before, preferred_element_type=F32)
    rank = jnp.sum(hot * count, axis=0, keepdims=True)
    to_ref[...] = own * CAP + rank.astype(I32)
    pos = pos_ref[...]
    here = pos // GPOOL == group
    rank = jnp.dot(here.astype(F32).astype(BF16), before, preferred_element_type=F32).astype(I32)
    rank = jnp.where(here, rank, -1)
    local = pos % GPOOL + 1
    high = (local // 32).astype(F32)
    low = (local % 32).astype(F32)
    r = lax.broadcasted_iota(I32, (CAP, GPOOL), 0)
    for g in range(GROUPS):
        pick = (rank[g : g + 1] == r).astype(F32).astype(BF16)
        pair = jnp.concatenate([high[g : g + 1], low[g : g + 1], jnp.zeros((6, GPOOL), F32)], axis=0)
        got = lax.dot_general(pair.astype(BF16), pick, (((1,), (1,)), ((), ())), preferred_element_type=F32)
        value = got[0:1] * 32.0 + got[1:2] - 1.0
        from_ref[:, g * CAP : (g + 1) * CAP] = value.astype(I32)


def pack_kernel(scal_ref, to_ref, got_ref, out_ref, all_ref):
    chip = scal_ref[0] // 2
    for k in range(QUADS):
        source = chip % QUADS + QUADS * k
        for i, off in enumerate(WINDOW):
            row = ((source + off + CHIPS) % CHIPS) * ROWS
            all_ref[pl.ds(pl.multiple_of(row, ROWS), ROWS), :] = got_ref[k, i * ROWS : (i + 1) * ROWS, :]
    rows = 256
    for i in range(GROUPS * CAP // rows):
        r = i * rows + lax.broadcasted_iota(I32, (rows, GPOOL), 0)
        pick = jnp.where(to_ref[...] == r, 1.0, 0.0).astype(BF16)
        out_ref[i * rows : (i + 1) * rows, :] = jnp.dot(pick, all_ref[...], preferred_element_type=F32).astype(BF16)


def place_kernel(from_ref, got_ref, out_ref):
    rows = 256
    for i in range(GPOOL // rows):
        r = i * rows + lax.broadcasted_iota(I32, (rows, GROUPS * CAP), 0)
        pick = jnp.where(from_ref[...] == r, 1.0, 0.0).astype(BF16)
        out_ref[i * rows : (i + 1) * rows, :] = jnp.dot(pick, got_ref[...], preferred_element_type=F32).astype(BF16)


def body(queries, keys, values, gamma, w_merge, grids, positions):
    me = lax.axis_index(MLP)
    core = me % 2
    scal = jnp.stack([me, core, lax.axis_index("grp"), me]).astype(I32)
    shape = jax.ShapeDtypeStruct

    def move(x, perm):
        return lax.ppermute(x, MLP, perm)

    grids = grids.T
    halves = rope(scal, grids, queries, keys, values)
    w_merge, halves = lax.optimization_barrier((w_merge, halves))
    cols = lax.all_gather(w_merge, "zq", axis=0)
    halves, cols = lax.optimization_barrier((halves, cols))
    cols = lax.all_gather(cols, "grp", axis=0)
    parts = []
    for own, oth in halves:
        up = move(own, SAME)
        across = move(oth, OPP)
        parts.append([own, up, across, move(oth, PART)])

    tables = pl.pallas_call(
        layout_kernel,
        out_shape=[pltpu.HBM((NB * BLK, HD), BF16)] * 2 + [pltpu.HBM((2 * ROWS, NB * BLK), BF16)],
        in_specs=[smem(), smem()],
        out_specs=[vmem()] * 3,
        compiler_params=params(16),
        name="layout",
    )(scal, grids)
    gains, _ = lax.optimization_barrier((jnp.broadcast_to(gamma[None, :], (2 * CHIPS, HD)), halves))
    gains = lax.all_to_all(gains, MLP, split_axis=0, concat_axis=0, tiled=True)
    gains = lax.dynamic_slice_in_dim(gains, core * CHIPS, CHIPS, 0).reshape(1, HALF).astype(F32)
    owns, tables = lax.optimization_barrier(([p[0] for p in parts], tables))
    pooled = []
    for chunk in range(CHUNKS):
        mid, edge = attend([owns[chunk]] + parts[chunk][1:], tables)
        pooled.append((mid, edge))
        if chunk == 0:
            positions, _ = lax.optimization_barrier((positions, mid))
            to, frm = pl.pallas_call(
                index_kernel,
                out_shape=[shape((1, GPOOL), I32), shape((1, GROUPS * CAP), I32)],
                in_specs=[smem(), vmem()],
                out_specs=[vmem(), vmem()],
                compiler_params=params(24),
                name="index",
            )(scal, positions.reshape(GROUPS, GPOOL))
            tables, to, frm, gains = lax.optimization_barrier((tables, to, frm, gains))
    mid, edge = (jnp.concatenate(half, axis=1) for half in zip(*pooled))
    rows = mid + move(edge, RING)
    rows = (rows.astype(F32) * gains).astype(BF16)
    below = move(rows, UP)
    above = move(rows, DOWN)
    last = move(below, UP)
    own = (below, rows, above, last)
    oth = [move(x, PART) for x in own]
    cols, _ = lax.optimization_barrier((cols, (below, above)))
    out = project(scal, own, oth, cols)
    out = lax.all_to_all(out, "zq", split_axis=0, concat_axis=0, tiled=True)

    out = pl.pallas_call(
        pack_kernel,
        out_shape=shape((GROUPS * CAP, HD), BF16),
        in_specs=[smem(), vmem(), vmem()],
        out_specs=vmem(),
        scratch_shapes=[pltpu.VMEM((GPOOL, HD), BF16)],
        compiler_params=params(24),
        name="pack",
    )(scal, to, out)
    out = lax.all_to_all(out, "grp", split_axis=0, concat_axis=0, tiled=True)
    return pl.pallas_call(
        place_kernel,
        out_shape=shape((GPOOL, HD), BF16),
        in_specs=[vmem(), vmem()],
        out_specs=vmem(),
        compiler_params=params(24),
        name="place",
    )(frm, out)


def solution(mesh):
    mesh = Mesh(mesh.devices.reshape(GROUPS, CHIPS // QUADS, QUADS, 2), ("grp",) + MLP)
    every = P(("grp",) + MLP, None)
    return jax.shard_map(
        body,
        mesh=mesh,
        in_specs=(every, every, every, P(MLP), P("grp", MLP), P("grp", None), P()),
        out_specs=P("grp", MLP),
        check_vma=False,
    )
```

```python
import math

import jax
import jax.numpy as jnp
from jax import lax
from jax.experimental import pallas as pl
from jax.experimental.pallas import tpu as pltpu
from jax.sharding import Mesh
from jax.sharding import PartitionSpec as P

HD = 128
HALF = 2048
IMGS = 16
BLK = 128
CHIPS = 16
CHUNKS = 2
HEADS = 8
WIDE = HEADS * HD
STEP = 4
NB = 4
ROWS = 64
CAP = 128
GROUPS = 16
GPOOL = 1024
SCALE = HD ** -0.5 / math.log(2.0)
F32 = jnp.float32
BF16 = jnp.bfloat16
I32 = jnp.int32
MLP = ("zq", "zr", "core")
WINDOW = (-1, 0, 1, -2)
QUADS = 4


def at(z, c):
    return (z % CHIPS) * 2 + c


SAME = [(at(z, 0), at(z - 1, 0)) for z in range(CHIPS)] + [(at(z, 1), at(z + 1, 1)) for z in range(CHIPS)]
OPP = [(at(z, 1), at(z - 1, 0)) for z in range(CHIPS)] + [(at(z, 0), at(z + 1, 1)) for z in range(CHIPS)]
RING = [(at(z, 0), at(z + 1, 0)) for z in range(CHIPS)] + [(at(z, 1), at(z - 1, 1)) for z in range(CHIPS)]
UP = [(at(z, c), at(z + 1, c)) for z in range(CHIPS) for c in range(2)]
DOWN = [(at(z, c), at(z - 1, c)) for z in range(CHIPS) for c in range(2)]
PART = [(at(z, c), at(z, 1 - c)) for z in range(CHIPS) for c in range(2)]


def vmem():
    return pl.BlockSpec(memory_space=pltpu.VMEM)


def smem():
    return pl.BlockSpec(memory_space=pltpu.SMEM)


def params(mib):
    return pltpu.CompilerParams(vmem_limit_bytes=mib << 20)


def cost(us):
    return pl.CostEstimate(flops=int(us * 1.15e9), bytes_accessed=int(us * 3.5e6), transcendentals=0)


def images_of(tok, grid_ref):
    image = jnp.where(tok < 0, -1, 0)
    first = jnp.zeros_like(tok)
    width = jnp.full_like(tok, grid_ref[1, 0])
    end = jnp.full_like(tok, grid_ref[0, 0] * grid_ref[1, 0])
    upto = jnp.int32(0)
    for n in range(IMGS):
        upto = upto + grid_ref[0, n] * grid_ref[1, n]
        past = tok >= upto
        image = jnp.where(past, n + 1, image)
        first = jnp.where(past, upto, first)
        if n + 1 < IMGS:
            width = jnp.where(past, grid_ref[1, n + 1], width)
            end = jnp.where(past, upto + grid_ref[0, n + 1] * grid_ref[1, n + 1], end)
        else:
            width = jnp.where(past, 2, width)
    return image, first, width, end


def divide(a, b):
    return jnp.floor((a.astype(F32) + 0.5) / b.astype(F32)).astype(I32)


def rope_kernel(scal_ref, grid_ref, q_ref, k_ref, v_ref, *refs):
    outs = refs[: 2 * CHUNKS]
    cos_ref, sin_ref = refs[2 * CHUNKS :]
    lane = lax.broadcasted_iota(I32, (BLK, HD), 1)
    low = (lane % 64) < 32
    step = pl.program_id(0)

    @pl.when(step == 0)
    def _():
        tok = scal_ref[0] * BLK + lax.broadcasted_iota(I32, (BLK, HD), 0)
        _, first, width, _ = images_of(tok, grid_ref)
        local = tok - first
        row = divide(local, width)
        col = local - row * width
        freq = jnp.exp((lane % 32).astype(F32) * (-math.log(100.0) / 32.0))
        ang = jnp.where(lane < 64, row, col).astype(F32) * freq
        cos_ref[...] = jnp.cos(ang)
        sin = jnp.sin(ang)
        sin_ref[...] = jnp.where(low, -sin, sin)

    def fill(out_ref):
        cos = cos_ref[...]
        sin = sin_ref[...]
        for h in range(HEADS):
            lanes = slice(h * HD, (h + 1) * HD)
            for i, ref in ((0, q_ref), (1, k_ref)):
                x = ref[:, lanes].astype(F32)
                swap = jnp.where(low, pltpu.roll(x, 96, 1), pltpu.roll(x, 32, 1))
                out_ref[i, :, lanes] = (x * cos + swap * sin).astype(BF16)
        out_ref[2] = v_ref[...]

    for i in range(2 * CHUNKS):

        @pl.when(step == i)
        def _(out_ref=outs[i]):
            fill(out_ref)


def rope(scal, grids, queries, keys, values):
    queries, keys, values = (pltpu.with_memory_space_constraint(x, pltpu.HBM) for x in (queries, keys, values))

    def src(i, scal_ref):
        half = jnp.where(i % 2 == 0, scal_ref[1], 1 - scal_ref[1])
        return (0, half * (HALF // WIDE) + i // 2)

    outs = pl.pallas_call(
        rope_kernel,
        out_shape=[jax.ShapeDtypeStruct((3, BLK, WIDE), BF16)] * (2 * CHUNKS),
        grid_spec=pltpu.PrefetchScalarGridSpec(
            num_scalar_prefetch=1,
            grid=(2 * CHUNKS,),
            in_specs=[smem()] + [pl.BlockSpec((BLK, WIDE), src)] * 3,
            out_specs=[pl.BlockSpec((3, BLK, WIDE), lambda i, _: (0, 0, 0))] * (2 * CHUNKS),
            scratch_shapes=[pltpu.VMEM((BLK, HD), F32)] * 2,
        ),
        compiler_params=params(24),
        cost_estimate=cost(6),
        name="rope",
    )(scal, grids, queries, keys, values)
    return [outs[2 * c : 2 * c + 2] for c in range(CHUNKS)]


def layout_kernel(scal_ref, grid_ref, qhot_ref, khot_ref, pool_ref):
    chip = scal_ref[0] // 2
    core = scal_ref[1]
    lo = chip * 2 * BLK
    hi = lo + 2 * BLK
    for i in range(NB):
        tok = lo + BLK * jnp.where(core == 0, i, 1 - i) + lax.broadcasted_iota(I32, (BLK, HD), 0)
        image, _, _, _ = images_of(tok, grid_ref)
        hot = image + 1 == lax.broadcasted_iota(I32, (BLK, HD), 1)
        qhot_ref[i * BLK : (i + 1) * BLK, :] = jnp.where(hot, 256.0, 0.0).astype(BF16)
        khot_ref[i * BLK : (i + 1) * BLK, :] = jnp.where(hot, 128.0, 0.0).astype(BF16)
    lane = lax.broadcasted_iota(I32, (8, NB * BLK), 1)
    place = lane // BLK
    tok = lo + lane % BLK + BLK * jnp.where(core == 0, place, 1 - place)
    image, first, width, end = images_of(tok, grid_ref)
    local = tok - first
    prow = divide(jnp.maximum(local, 0), width)
    pcol = local - prow * width
    target = first // 4 + (prow // 2) * (width // 2) + pcol // 2
    begins = (first >= lo) & (first < hi)
    ends = (end > lo) & (end <= hi)
    owned = jnp.where(core == 0, begins.astype(I32), ends.astype(I32)) > 0
    target = jnp.where(owned & (image >= 0) & (image < IMGS), target, -1)[:1]
    r = lax.broadcasted_iota(I32, (2 * ROWS, NB * BLK), 0)
    far = jnp.where(core == 0, ROWS, -ROWS)
    mine = chip * ROWS + jnp.where(r < ROWS, r, r - ROWS + far)
    pool_ref[...] = jnp.where((target == mine) & (target >= 0), 1.0, 0.0).astype(BF16)


def attend_kernel(a_ref, c_ref, d_ref, b_ref, qhot_ref, khot_ref, pool_ref, mid_ref, edge_ref):
    refs = (a_ref, b_ref, c_ref, d_ref)
    pairs = NB // 2
    ones = jnp.ones((16, NB * BLK), BF16)
    nt = (((1,), (1,)), ((), ()))

    def score(h, i):
        lanes = slice(h * HD, (h + 1) * HD)
        keys = jnp.concatenate([ref[1, :, lanes] for ref in refs], axis=0)
        keys = jnp.concatenate([keys, khot_ref[...]], axis=1)
        q = jnp.concatenate([ref[0, :, lanes] for ref in refs[2 * i : 2 * i + 2]], axis=0)
        q = jnp.concatenate([q, qhot_ref[i * 2 * BLK : (i + 1) * 2 * BLK, :]], axis=1)
        return lax.dot_general(keys, q, nt, preferred_element_type=F32)

    def mix(h, s):
        lanes = slice(h * HD, (h + 1) * HD)
        e = jnp.exp2((s - jnp.max(s, axis=0, keepdims=True)) * SCALE).astype(BF16)
        vals = jnp.concatenate([ref[2, :, lanes] for ref in refs], axis=0)
        o = jnp.dot(jnp.concatenate([vals.T, ones], axis=0), e, preferred_element_type=F32)
        return (o[:HD] / o[HD : HD + 1]).astype(BF16)

    order = [(h, i) for h in range(STEP) for i in range(pairs)]
    later = score(*order[0])
    done = []
    for t, (h, i) in enumerate(order):
        now = later
        if t + 1 < len(order):
            later = score(*order[t + 1])
        done.append(mix(h, now))
        if len(done) == pairs:
            branch = jnp.concatenate(done, axis=1)
            done = []
            pooled = lax.dot_general(pool_ref[...], branch, nt, preferred_element_type=F32)
            pooled = (0.25 * pooled).astype(BF16)
            lanes = slice(h * HD, (h + 1) * HD)
            mid_ref[:, lanes] = pooled[:ROWS]
            edge_ref[:, lanes] = pooled[ROWS:]


def attend(parts, tables):
    part = pl.BlockSpec((3, BLK, STEP * HD), lambda h: (0, 0, h))
    tables = [pltpu.with_memory_space_constraint(t, pltpu.HBM) for t in tables]
    whole = [pl.BlockSpec(t.shape, lambda h: (0, 0)) for t in tables]
    return pl.pallas_call(
        attend_kernel,
        grid=(HEADS // STEP,),
        out_shape=[jax.ShapeDtypeStruct((ROWS, WIDE), BF16)] * 2,
        in_specs=[part] * NB + whole,
        out_specs=[pl.BlockSpec((ROWS, STEP * HD), lambda h: (0, h))] * 2,
        compiler_params=params(32),
        cost_estimate=cost(6),
        name="attend",
    )(*parts, *tables)


def project_kernel(scal_ref, *refs):
    w_own_ref, w_oth_ref, out_ref = refs[-3:]
    own = jnp.concatenate([ref[...] for ref in refs[:NB]], axis=0)
    oth = jnp.concatenate([ref[...] for ref in refs[NB : 2 * NB]], axis=0)

    def pair(ref):
        return jnp.concatenate([ref[:, i].reshape(HALF, HD) for i in range(2)], axis=1)

    total = jnp.dot(own, pair(w_own_ref), preferred_element_type=F32)
    total += jnp.dot(oth, pair(w_oth_ref), preferred_element_type=F32)
    for i in range(2):
        out_ref[i] = total[:, i * HD : (i + 1) * HD].astype(BF16)


def project(scal, own, oth, cols):
    rows = NB * ROWS
    half = (GROUPS // 2, 2, 2 * BLK, HD)
    cols = pltpu.with_memory_space_constraint(cols, pltpu.HBM)
    return pl.pallas_call(
        project_kernel,
        out_shape=jax.ShapeDtypeStruct((QUADS, rows, HD), BF16),
        grid_spec=pltpu.PrefetchScalarGridSpec(
            num_scalar_prefetch=1,
            grid=(QUADS // 2,),
            in_specs=[pl.BlockSpec((ROWS, HALF), lambda j, _: (0, 0))] * (2 * NB)
            + [
                pl.BlockSpec(half, lambda j, s: (s[1], j, 0, 0)),
                pl.BlockSpec(half, lambda j, s: (1 - s[1], j, 0, 0)),
            ],
            out_specs=pl.BlockSpec((2, rows, HD), lambda j, _: (j, 0, 0)),
        ),
        compiler_params=params(24),
        cost_estimate=cost(4),
        name="project",
    )(scal, *own, *oth, cols, cols)


def index_kernel(scal_ref, pos_ref, to_ref, from_ref):
    group = scal_ref[2]
    i = lax.broadcasted_iota(I32, (GPOOL, GPOOL), 0)
    j = lax.broadcasted_iota(I32, (GPOOL, GPOOL), 1)
    before = jnp.where(i < j, 1.0, 0.0).astype(BF16)
    own = pos_ref[pl.ds(group, 1), :] // GPOOL
    hot = (own == lax.broadcasted_iota(I32, (GROUPS, GPOOL), 0)).astype(F32)
    count = jnp.dot(hot.astype(BF16), before, preferred_element_type=F32)
    rank = jnp.sum(hot * count, axis=0, keepdims=True)
    to_ref[...] = own * CAP + rank.astype(I32)
    pos = pos_ref[...]
    here = pos // GPOOL == group
    rank = jnp.dot(here.astype(F32).astype(BF16), before, preferred_element_type=F32).astype(I32)
    rank = jnp.where(here, rank, -1)
    local = pos % GPOOL + 1
    high = (local // 32).astype(F32)
    low = (local % 32).astype(F32)
    r = lax.broadcasted_iota(I32, (CAP, GPOOL), 0)
    for g in range(GROUPS):
        pick = (rank[g : g + 1] == r).astype(F32).astype(BF16)
        pair = jnp.concatenate([high[g : g + 1], low[g : g + 1], jnp.zeros((6, GPOOL), F32)], axis=0)
        got = lax.dot_general(pair.astype(BF16), pick, (((1,), (1,)), ((), ())), preferred_element_type=F32)
        value = got[0:1] * 32.0 + got[1:2] - 1.0
        from_ref[:, g * CAP : (g + 1) * CAP] = value.astype(I32)


def pack_kernel(scal_ref, to_ref, got_ref, out_ref, all_ref):
    chip = scal_ref[0] // 2
    for k in range(QUADS):
        source = chip % QUADS + QUADS * k
        for i, off in enumerate(WINDOW):
            row = ((source + off + CHIPS) % CHIPS) * ROWS
            all_ref[pl.ds(pl.multiple_of(row, ROWS), ROWS), :] = got_ref[k, i * ROWS : (i + 1) * ROWS, :]
    rows = 256
    for i in range(GROUPS * CAP // rows):
        r = i * rows + lax.broadcasted_iota(I32, (rows, GPOOL), 0)
        pick = jnp.where(to_ref[...] == r, 1.0, 0.0).astype(BF16)
        out_ref[i * rows : (i + 1) * rows, :] = jnp.dot(pick, all_ref[...], preferred_element_type=F32).astype(BF16)


def place_kernel(from_ref, got_ref, out_ref):
    rows = 256
    for i in range(GPOOL // rows):
        r = i * rows + lax.broadcasted_iota(I32, (rows, GROUPS * CAP), 0)
        pick = jnp.where(from_ref[...] == r, 1.0, 0.0).astype(BF16)
        out_ref[i * rows : (i + 1) * rows, :] = jnp.dot(pick, got_ref[...], preferred_element_type=F32).astype(BF16)


def body(queries, keys, values, gamma, w_merge, grids, positions):
    me = lax.axis_index(MLP)
    core = me % 2
    scal = jnp.stack([me, core, lax.axis_index("grp"), me]).astype(I32)
    shape = jax.ShapeDtypeStruct

    def move(x, perm):
        return lax.ppermute(x, MLP, perm)

    grids = grids.T
    halves = rope(scal, grids, queries, keys, values)
    w_merge, halves = lax.optimization_barrier((w_merge, halves))
    cols = lax.all_gather(w_merge, "zq", axis=0)
    halves, cols = lax.optimization_barrier((halves, cols))
    cols = lax.all_gather(cols, "grp", axis=0)
    parts = []
    for own, oth in halves:
        up = move(own, SAME)
        across = move(oth, OPP)
        parts.append([own, up, across, move(oth, PART)])

    tables = pl.pallas_call(
        layout_kernel,
        out_shape=[pltpu.HBM((NB * BLK, HD), BF16)] * 2 + [pltpu.HBM((2 * ROWS, NB * BLK), BF16)],
        in_specs=[smem(), smem()],
        out_specs=[vmem()] * 3,
        compiler_params=params(16),
        name="layout",
    )(scal, grids)
    gains, _ = lax.optimization_barrier((jnp.broadcast_to(gamma[None, :], (2 * CHIPS, HD)), halves))
    gains = lax.all_to_all(gains, MLP, split_axis=0, concat_axis=0, tiled=True)
    gains = lax.dynamic_slice_in_dim(gains, core * CHIPS, CHIPS, 0).reshape(1, HALF).astype(F32)
    owns, tables = lax.optimization_barrier(([p[0] for p in parts], tables))
    pooled = []
    for chunk in range(CHUNKS):
        mid, edge = attend([owns[chunk]] + parts[chunk][1:], tables)
        pooled.append((mid, edge))
        if chunk == 0:
            positions, _ = lax.optimization_barrier((positions, mid))
            to, frm = pl.pallas_call(
                index_kernel,
                out_shape=[shape((1, GPOOL), I32), shape((1, GROUPS * CAP), I32)],
                in_specs=[smem(), vmem()],
                out_specs=[vmem(), vmem()],
                compiler_params=params(24),
                name="index",
            )(scal, positions.reshape(GROUPS, GPOOL))
            tables, to, frm, gains = lax.optimization_barrier((tables, to, frm, gains))
    mid, edge = (jnp.concatenate(half, axis=1) for half in zip(*pooled))
    rows = mid + move(edge, RING)
    rows = (rows.astype(F32) * gains).astype(BF16)
    below = move(rows, UP)
    above = move(rows, DOWN)
    last = move(below, UP)
    own = (below, rows, above, last)
    oth = [move(x, PART) for x in own]
    cols, _ = lax.optimization_barrier((cols, (below, above)))
    out = project(scal, own, oth, cols)
    out = lax.all_to_all(out, "zq", split_axis=0, concat_axis=0, tiled=True)

    out = pl.pallas_call(
        pack_kernel,
        out_shape=shape((GROUPS * CAP, HD), BF16),
        in_specs=[smem(), vmem(), vmem()],
        out_specs=vmem(),
        scratch_shapes=[pltpu.VMEM((GPOOL, HD), BF16)],
        compiler_params=params(24),
        name="pack",
    )(scal, to, out)
    out = lax.all_to_all(out, "grp", split_axis=0, concat_axis=0, tiled=True)
    return pl.pallas_call(
        place_kernel,
        out_shape=shape((GPOOL, HD), BF16),
        in_specs=[vmem(), vmem()],
        out_specs=vmem(),
        compiler_params=params(24),
        name="place",
    )(frm, out)


def solution(mesh):
    mesh = Mesh(mesh.devices.reshape(GROUPS, CHIPS // QUADS, QUADS, 2), ("grp",) + MLP)
    every = P(("grp",) + MLP, None)
    return jax.shard_map(
        body,
        mesh=mesh,
        in_specs=(every, every, every, P(MLP), P("grp", MLP), P("grp", None), P()),
        out_specs=P("grp", MLP),
        check_vma=False,
    )
```
